256 devices in a mesh: pl: 16 (over y, x), xs: 16 (over z, core).
Axes of the slice: x: 4, y: 4, z: 8, core: 2. Of those that a mesh axis runs over, the one named last changes fastest.
Arguments:
- source: float32 [512, 16, 2048], P('xs', None, 'pl'), may hold values from -6 to 6
- eastward_rate: float32 [512, 16, 2048], P('xs', None, 'pl'), may hold values from 300 to 6000
- northward_rate: float32 [512, 16, 2048], P('xs', None, 'pl'), may hold values from 300 to 6000
- vertical_rate: float32 [512, 16, 2048], P('xs', None, 'pl'), may hold values from 0.5 to 20
- amplitude: float32 [512, 16, 2048], P('xs', None, 'pl'), may hold values from 300 to 3000
Outputs:
- smoothed: float32 [512, 16, 2048], P('xs', None, 'pl')
The draws below stay inside these ranges and needn't reach their ends.
All inputs are finite; a program needn't handle non-finite values.
Results may differ from the reference program's by a relative error of at most 0.0003.
Values sent between devices are 32-bit elements; how exact they have to be, the bound alone decides.
A program may use at most 128 MiB of HBM per device.

```python
import math
import jax
import jax.numpy as jnp
from jax import lax

NZ = 16
NX = 512
NY = 2048


def draw_source(key, part):
    extent = (NX, NZ, NY)
    return jnp.clip(jax.random.normal(key, extent, jnp.float32), -6.0, 6.0)


def block_scale(rng, dims, cuts, least, top_value):
    level = 1.0
    for dim, shards_of in cuts:
        steps = jax.random.uniform(jax.random.fold_in(jax.random.fold_in(rng, 6), dim), (shards_of,), jnp.float32, least / len(cuts), top_value / len(cuts))
        level = level * jnp.repeat(jnp.exp(steps), dims[dim] // shards_of).reshape((-1,) + (1,) * (len(dims) - 1 - dim))
    return level


def setup_inputs(seed: int = 0) -> dict:
    splits = jax.random.split(jax.random.key(seed), 6)
    return {
        "source": draw_source(jax.random.fold_in(splits[5], 71), 0),
        "eastward_rate": jnp.clip(jnp.exp(math.log(6000.0) - 2.9957323 * jax.random.uniform(splits[1], (NX, NZ, NY), jnp.float32) ** block_scale(splits[1], (NX, NZ, NY), ((0, 16), (2, 16)), -0.2, 0.2)), 300.0, 6000.0),
        "northward_rate": jnp.clip(jnp.exp(math.log(6000.0) - 2.9957323 * jax.random.uniform(splits[2], (NX, NZ, NY), jnp.float32) ** block_scale(splits[2], (NX, NZ, NY), ((0, 16), (2, 16)), -0.2, 0.2)), 300.0, 6000.0),
        "vertical_rate": jnp.clip(jnp.exp(math.log(20.0) - 3.6888795 * jax.random.uniform(splits[3], (NX, NZ, NY), jnp.float32) ** block_scale(splits[3], (NX, NZ, NY), ((0, 16), (2, 16)), -0.2, 0.2)), 0.5, 20.0),
        "amplitude": jnp.clip(jnp.exp(math.log(3000.0) - 2.3025851 * jax.random.uniform(splits[4], (NX, NZ, NY), jnp.float32) ** block_scale(splits[4], (NX, NZ, NY), ((0, 16), (2, 16)), -0.2, 0.2)), 300.0, 3000.0),
    }


def line_solve(values, coefficient, dimension):
    moved_values = jnp.moveaxis(values, dimension, -1)
    moved_rate = jnp.moveaxis(coefficient, dimension, -1)
    length = moved_values.shape[-1]
    position = jnp.arange(length)
    sub_band = jnp.where(position > 0, -moved_rate, 0.0)
    super_band = jnp.where(position < length - 1, -moved_rate, 0.0)
    centre = 1.0 + 2.0 * moved_rate
    solved = lax.linalg.tridiagonal_solve(sub_band, centre, super_band, moved_values[..., None])[..., 0]
    return jnp.moveaxis(solved, -1, dimension)

def reference(source, eastward_rate, northward_rate, vertical_rate, amplitude):
    values = line_solve(source, vertical_rate, 1)
    values = line_solve(values, northward_rate, 2)
    values = line_solve(values, eastward_rate, 0)
    values = line_solve(values, eastward_rate, 0)
    values = line_solve(values, northward_rate, 2)
    values = line_solve(values, vertical_rate, 1)
    return amplitude * values
```

```python
import functools

import jax
import jax.numpy as jnp
from jax import lax
from jax.experimental import pallas as pl
from jax.experimental.pallas import tpu as pltpu
from jax.sharding import PartitionSpec as P

MESH = pl.DeviceIdType.MESH
LANES = 128
HIGHEST = lax.Precision.HIGHEST


def reduced_factors(count, load, store):
    one = None
    b = None
    forward = []
    for j in range(count):
        left, right, shared = load(j)
        if b is None:
            b = jnp.zeros_like(left)
            one = jnp.ones_like(left)
        store("b", j, b)
        a1 = shared / (one - left * b)
        a2 = a1 * b
        store("a1", j, a1)
        store("a2", j, a2)
        b = right + a2 * shared
        forward.append(b)
    store("b", count, b)
    d = jnp.zeros_like(b)
    store("d", count, d)
    store("g", count, one)
    for j in reversed(range(count)):
        left, right, shared = load(j)
        c1 = shared / (one - right * d)
        c2 = c1 * d
        store("c1", j, c1)
        store("c2", j, c2)
        d = left + c2 * shared
        store("d", j, d)
        before = forward[j - 1] if j else jnp.zeros_like(d)
        store("g", j, one / (one - before * d))


def running(count, first, second, value, phi, psi, keep, emit):
    total = None
    for i in reversed(range(count)):
        term = second(i) * value(i)
        if total is None:
            total = jnp.zeros_like(term)
        keep(i, total)
        total = total + term
    total = jnp.zeros_like(total)
    for i in range(count):
        total = total + first(i) * value(i)
        emit(i, psi(i) * total + phi(i) * keep(i))


def kernel(
    nx, nz, n_pl, n_xs,
    source_hbm, vertical_hbm, north_hbm, east_hbm, out_ref,
    source, vertical, north, east,
    z_phi, z_psi, z_first, z_second,
    y_rate, y_phi, y_psi, y_first, y_second, y_value, y_part,
    x_phi, x_psi, x_phi2, x_psi2, x_first, x_second, x_first2, x_second2,
    x_part, x_part2, plane, hold,
    y_coef, y_ends, y_ends2, x_coef, x_coef_in, x_ends, x_ends_in, x_back, x_back_in,
    y_fac, y_scan, x_fac,
    load_sem, send_sem, recv_sem,
):
    lines = nx * nz
    blocks = lines // LANES
    pl_me, xs_me = lax.axis_index("pl"), lax.axis_index("xs")

    loads = []
    for slot, (hbm, vmem) in enumerate(
        ((north_hbm, north), (vertical_hbm, vertical), (source_hbm, source), (east_hbm, east))
    ):
        copy = pltpu.make_async_copy(hbm, vmem, load_sem.at[slot])
        copy.start()
        loads.append(copy)

    barrier = pltpu.get_barrier_semaphore()
    for o in range(1, n_pl):
        pl.semaphore_signal(barrier, 1, device_id={"pl": lax.rem(pl_me + o, n_pl)}, device_id_type=MESH)
    for o in range(1, n_xs):
        pl.semaphore_signal(barrier, 1, device_id={"xs": lax.rem(xs_me + o, n_xs)}, device_id_type=MESH)

    def share(axis, slot, pick, landing):
        count, me = (n_pl, pl_me) if axis == "pl" else (n_xs, xs_me)
        for o in range(1, count):
            peer = lax.rem(me + o, count)
            pltpu.make_async_remote_copy(
                src_ref=pick(peer),
                dst_ref=landing.at[me],
                send_sem=send_sem.at[slot],
                recv_sem=recv_sem.at[slot],
                device_id={axis: peer},
                device_id_type=MESH,
            ).start()

    def arrived(slot, landing, sem=None):
        count = landing.shape[0]
        if count > 1:
            whole = landing.at[pl.ds(0, count - 1)]
            sem = recv_sem if sem is None else sem
            pltpu.make_async_copy(whole, whole, sem.at[slot]).wait()

    def rows(b):
        return pl.ds(b * LANES, LANES)

    def across(y):
        return pl.ds(y, blocks, stride=LANES)

    loads[0].wait()
    for b in range(blocks):
        y_rate[rows(b)] = (1.0 / north[rows(b)]).T

    def y_sweep(i, carry):
        phi, phi_step, psi, psi_step = carry
        y_phi[across(i)] = phi
        y_psi[across(LANES - 1 - i)] = psi
        phi_step = phi_step + phi * y_rate[across(i)]
        psi_step = psi_step + psi * y_rate[across(LANES - 1 - i)]
        return phi + phi_step, phi_step, psi + psi_step, psi_step

    unit = jnp.ones((blocks, LANES), jnp.float32)
    y_phi_end = lax.fori_loop(0, LANES, y_sweep, (unit, unit, unit, unit), unroll=8)[0]
    y_inv = 1.0 / y_phi_end
    hold[pl.ds(0, blocks)] = y_inv
    for b in range(blocks):
        inv = hold[b:b + 1]
        scaled = y_rate[rows(b)] * inv
        y_first[rows(b)] = y_phi[rows(b)] * scaled
        y_second[rows(b)] = y_psi[rows(b)] * scaled
    y_coef[pl_me, 0] = y_psi[across(0)] * y_inv
    y_coef[pl_me, 1] = y_phi[across(LANES - 1)] * y_inv
    y_coef[pl_me, 2] = y_inv

    pl.semaphore_wait(barrier, n_pl + n_xs - 2)
    share("pl", 0, lambda peer: y_coef.at[pl_me], y_coef)

    def level(z):
        return pl.ds(z, nx, stride=nz)

    loads[1].wait()
    phi = jnp.ones((nx, LANES), jnp.float32)
    phi_step = psi = psi_step = phi
    for z in range(nz):
        back = nz - 1 - z
        up, down = 1.0 / vertical[level(z)], 1.0 / vertical[level(back)]
        z_phi[z] = phi
        z_psi[back] = psi
        z_first[z] = phi * up
        z_second[back] = psi * down
        phi_step = phi_step + phi * up
        psi_step = psi_step + psi * down
        phi = phi + phi_step
        psi = psi + psi_step
    z_inv = 1.0 / phi
    for z in range(nz):
        z_first[z] = z_first[z] * z_inv
        z_second[z] = z_second[z] * z_inv

    def z_solve(read, write):
        def keep(z, value=None):
            if value is None:
                return x_part2[pl.ds(z * nx, nx)]
            x_part2[pl.ds(z * nx, nx)] = value

        running(nz, lambda z: z_first[z], lambda z: z_second[z], read, lambda z: z_phi[z], lambda z: z_psi[z], keep, write)

    loads[2].wait()

    def to_plane(z, value):
        plane[level(z)] = value

    z_solve(lambda z: source[level(z)], to_plane)

    low = lax.broadcasted_iota(jnp.int32, (LANES, LANES), 0)
    high = lax.broadcasted_iota(jnp.int32, (LANES, LANES), 1)
    upto = jnp.where(high <= low, 1.0, 0.0)
    beyond = jnp.where(high > low, 1.0, 0.0)

    def y_send(slot, ends):
        for b in range(blocks):
            value = plane[rows(b)].T
            second = y_second[rows(b)] * value
            first = y_first[rows(b)] * value
            y_value[rows(b)] = first
            y_part[rows(b)] = second
            ends[pl_me, 0, b:b + 1] = jnp.sum(second, axis=0, keepdims=True)
            ends[pl_me, 1, b:b + 1] = jnp.sum(first, axis=0, keepdims=True)
        share("pl", slot, lambda peer: ends.at[pl_me], ends)

    def y_local():
        for b in range(blocks):
            below = jnp.dot(upto, y_value[rows(b)], precision=HIGHEST, preferred_element_type=jnp.float32)
            above = jnp.dot(beyond, y_part[rows(b)], precision=HIGHEST, preferred_element_type=jnp.float32)
            y_part[rows(b)] = y_psi[rows(b)] * below + y_phi[rows(b)] * above

    def y_finish(slot, ends):
        arrived(slot, ends)
        a = c = jnp.zeros((blocks, LANES), jnp.float32)
        y_scan[0, 0] = a
        y_scan[1, n_pl] = c
        for j in range(n_pl):
            k = n_pl - 1 - j
            a = ends[j, 1] + y_fac[2, j] * ends[j, 0] + y_fac[1, j] * a
            c = ends[k, 0] + y_fac[4, k] * ends[k, 1] + y_fac[3, k] * c
            y_scan[0, j + 1] = a
            y_scan[1, k] = c
        a_here, a_next = y_scan[0, pl_me], y_scan[0, pl_me + 1]
        c_here, c_next = y_scan[1, pl_me], y_scan[1, pl_me + 1]
        outside_low = (a_here + y_fac[0, pl_me] * c_here) * y_fac[6, pl_me]
        outside_high = (c_next + y_fac[5, pl_me + 1] * a_next) * y_fac[6, pl_me + 1]
        inv = y_coef[pl_me, 2]
        hold[pl.ds(0, blocks)] = outside_low * inv
        hold[pl.ds(blocks, blocks)] = outside_high * inv
        for b in range(blocks):
            solved = (
                y_part[rows(b)]
                + y_psi[rows(b)] * hold[b:b + 1]
                + y_phi[rows(b)] * hold[blocks + b:blocks + b + 1]
            )
            plane[rows(b)] = solved.T

    y_send(1, y_ends)

    def step(i):
        return pl.ds(i * nz, nz)

    loads[3].wait()
    phi = jnp.ones((nz, LANES), jnp.float32)
    phi_step = psi = psi_step = phi
    for i in range(nx):
        back = nx - 1 - i
        up, down = 1.0 / east[step(i)], 1.0 / east[step(back)]
        x_phi[step(i)] = phi
        x_psi[step(back)] = psi
        x_first[step(i)] = phi * up
        x_second[step(back)] = psi * down
        phi_step = phi_step + phi * up
        psi_step = psi_step + psi * down
        phi = phi + phi_step
        psi = psi + psi_step
    x_inv = 1.0 / phi
    for i in range(nx):
        x_first[step(i)] = x_first[step(i)] * x_inv
        x_second[step(i)] = x_second[step(i)] * x_inv

    def x_solve(read, write):
        def keep(i, value=None):
            if value is None:
                return x_part2[step(i)]
            x_part2[step(i)] = value

        running(
            nx, lambda i: x_first[step(i)], lambda i: x_second[step(i)], read,
            lambda i: x_phi[step(i)], lambda i: x_psi[step(i)], keep, write,
        )

    def into(ref):
        def write(i, value):
            ref[step(i)] = value

        return write

    x_solve(lambda i: x_phi[step(i)], into(x_phi2))
    x_solve(lambda i: x_psi[step(i)], into(x_psi2))
    for i in range(nx):
        scaled = x_inv * (1.0 / east[step(i)])
        x_first2[step(i)] = x_phi2[step(i)] * scaled
        x_second2[step(i)] = x_psi2[step(i)] * scaled
    last = step(nx - 1)
    x_coef[:, 0] = x_psi[step(0)] * x_inv
    x_coef[:, 1] = x_phi[last] * x_inv
    x_coef[:, 2] = x_inv
    x_coef[:, 3] = x_psi2[step(0)] * x_inv
    x_coef[:, 4] = x_phi2[last] * x_inv
    x_coef[:, 5] = x_phi2[step(0)] * x_inv
    x_coef[:, 6] = x_inv
    x_coef[:, 7] = x_inv
    share("xs", 2, lambda peer: x_coef.at[peer], x_coef_in)
    x_coef_in[xs_me] = x_coef[xs_me]

    names = {"b": 0, "a1": 1, "a2": 2, "c1": 3, "c2": 4, "d": 5, "g": 6}
    arrived(0, y_coef)

    def y_store(name, j, value):
        y_fac[names[name], j] = value

    reduced_factors(n_pl, lambda j: (y_coef[j, 0], y_coef[j, 1], y_coef[j, 2]), y_store)
    y_local()
    y_finish(1, y_ends)

    p0 = pn = q0 = qn = jnp.zeros((nz, LANES), jnp.float32)
    for i in range(nx):
        value = plane[step(i)]
        p0 = p0 + x_second[step(i)] * value
        pn = pn + x_first[step(i)] * value
        q0 = q0 + x_second2[step(i)] * value
        qn = qn + x_first2[step(i)] * value
    x_ends[:, 0] = p0
    x_ends[:, 1] = pn
    x_ends[:, 2] = q0
    x_ends[:, 3] = qn
    share("xs", 3, lambda peer: x_ends.at[peer], x_ends_in)
    x_ends_in[xs_me] = x_ends[xs_me]

    arrived(2, x_coef_in)

    def x_store(name, j, value):
        x_fac[names[name], j:j + 1] = value

    reduced_factors(
        n_xs, lambda j: (x_coef_in[j, 0:1], x_coef_in[j, 1:2], x_coef_in[j, 2:3]), x_store
    )
    x_solve(lambda i: plane[step(i)], into(x_part))

    arrived(3, x_ends_in)

    def fac(name, j):
        return x_fac[names[name], j:j + 1]

    def x_reduced(ends):
        a = c = jnp.zeros((1, LANES), jnp.float32)
        lefts, rights = [a], [c]
        for j in range(n_xs):
            k = n_xs - 1 - j
            a = ends[j][1] + fac("a2", j) * ends[j][0] + fac("a1", j) * a
            c = ends[k][0] + fac("c2", k) * ends[k][1] + fac("c1", k) * c
            lefts.append(a)
            rights.append(c)
        rights = rights[::-1]
        lows = [(lefts[j] + fac("b", j) * rights[j]) * fac("g", j) for j in range(n_xs)]
        highs = [
            (rights[j + 1] + fac("d", j + 1) * lefts[j + 1]) * fac("g", j + 1) for j in range(n_xs)
        ]
        return lows, highs

    lows, highs = x_reduced([(x_ends_in[j, 0:1], x_ends_in[j, 1:2]) for j in range(n_xs)])
    again = []
    for j in range(n_xs):
        left, right, shared = x_coef_in[j, 3:4], x_coef_in[j, 4:5], x_coef_in[j, 5:6]
        again.append(
            (
                x_ends_in[j, 2:3] + left * lows[j] + shared * highs[j],
                x_ends_in[j, 3:4] + shared * lows[j] + right * highs[j],
            )
        )
    lows2, highs2 = x_reduced(again)
    for j in range(n_xs):
        inv = x_coef_in[j, 2:3]
        x_back[j, 0:1] = lows[j] * inv
        x_back[j, 1:2] = highs[j] * inv
        x_back[j, 2:3] = lows2[j] * inv
        x_back[j, 3:4] = highs2[j] * inv
    share("xs", 4, lambda peer: x_back.at[peer], x_back_in)
    x_back_in[xs_me] = x_back[xs_me]

    x_solve(lambda i: x_part[step(i)], into(x_part))
    arrived(4, x_back_in)
    low1, high1, low2, high2 = (x_back_in[:, q] for q in range(4))
    for i in range(nx):
        plane[step(i)] = (
            x_part[step(i)]
            + x_psi2[step(i)] * low1
            + x_phi2[step(i)] * high1
            + x_psi[step(i)] * low2
            + x_phi[step(i)] * high2
        )

    y_send(5, y_ends2)
    y_local()
    y_finish(5, y_ends2)

    def to_out(z, value):
        out_ref[level(z)] = value

    z_solve(lambda z: plane[level(z)], to_out)

    arrived(0, y_coef, send_sem)
    arrived(1, y_ends, send_sem)
    arrived(2, x_coef_in, send_sem)
    arrived(3, x_ends_in, send_sem)
    arrived(4, x_back_in, send_sem)
    arrived(5, y_ends2, send_sem)


def shards(n_pl, n_xs, source, eastward_rate, northward_rate, vertical_rate, amplitude):
    nx, nz, ny = source.shape
    lines = nx * nz
    blocks = lines // LANES
    flat = lambda array: array.reshape(lines, ny)
    field = pltpu.VMEM((lines, LANES), jnp.float32)
    column = pltpu.VMEM((nz, nx, LANES), jnp.float32)
    vmem = lambda *shape: pltpu.VMEM(shape, jnp.float32)
    second = pl.pallas_call(
        functools.partial(kernel, nx, nz, n_pl, n_xs),
        out_shape=jax.ShapeDtypeStruct((lines, ny), jnp.float32),
        in_specs=[pl.BlockSpec(memory_space=pl.ANY)] * 4,
        out_specs=pl.BlockSpec(memory_space=pltpu.VMEM),
        scratch_shapes=[field] * 4
        + [column] * 4
        + [field] * 7
        + [field] * 8
        + [field] * 3
        + [vmem(2 * blocks, LANES)]
        + [
            vmem(n_pl, 3, blocks, LANES),
            vmem(n_pl, 2, blocks, LANES),
            vmem(n_pl, 2, blocks, LANES),
            vmem(n_xs, 8, LANES),
            vmem(n_xs, 8, LANES),
            vmem(n_xs, 4, LANES),
            vmem(n_xs, 4, LANES),
            vmem(n_xs, 4, LANES),
            vmem(n_xs, 4, LANES),
            vmem(7, n_pl + 1, blocks, LANES),
            vmem(2, n_pl + 1, blocks, LANES),
            vmem(7, n_xs + 1, LANES),
            pltpu.SemaphoreType.DMA((4,)),
            pltpu.SemaphoreType.DMA((6,)),
            pltpu.SemaphoreType.DMA((6,)),
        ],
        compiler_params=pltpu.CompilerParams(
            collective_id=0, has_side_effects=True, vmem_limit_bytes=40 * 1024 * 1024
        ),
        name="adi",
    )(flat(source), flat(vertical_rate), flat(northward_rate), flat(eastward_rate))
    return amplitude * second.reshape(nx, nz, ny)


def solution(mesh):
    spec = P("xs", None, "pl")
    return jax.shard_map(
        functools.partial(shards, mesh.shape["pl"], mesh.shape["xs"]),
        mesh=mesh,
        in_specs=(spec,) * 5,
        out_specs=spec,
        check_vma=False,
    )
```

```python
import functools
import math

import jax
import jax.numpy as jnp
from jax import lax
from jax.experimental import pallas as pl
from jax.experimental.pallas import tpu as pltpu
from jax.sharding import PartitionSpec as P

MESH = pl.DeviceIdType.MESH
LANES = 128
HIGHEST = lax.Precision.HIGHEST


def reduced_factors(count, load, store):
    one = None
    b = None
    forward = []
    for j in range(count):
        left, right, shared = load(j)
        if b is None:
            b = jnp.zeros_like(left)
            one = jnp.ones_like(left)
        store("b", j, b)
        a1 = shared / (one - left * b)
        a2 = a1 * b
        store("a1", j, a1)
        store("a2", j, a2)
        b = right + a2 * shared
        forward.append(b)
    store("b", count, b)
    d = jnp.zeros_like(b)
    store("d", count, d)
    store("g", count, one)
    for j in reversed(range(count)):
        left, right, shared = load(j)
        c1 = shared / (one - right * d)
        c2 = c1 * d
        store("c1", j, c1)
        store("c2", j, c2)
        d = left + c2 * shared
        store("d", j, d)
        before = forward[j - 1] if j else jnp.zeros_like(d)
        store("g", j, one / (one - before * d))


def running(count, first, second, value, phi, psi, keep, emit):
    total = None
    for i in reversed(range(count)):
        term = second(i) * value(i)
        if total is None:
            total = jnp.zeros_like(term)
        keep(i, total)
        total = total + term
    total = jnp.zeros_like(total)
    for i in range(count):
        total = total + first(i) * value(i)
        emit(i, psi(i) * total + phi(i) * keep(i))


def kernel(
    nx, nz, n_pl, n_xs,
    source_hbm, vertical_hbm, north_hbm, east_hbm, out_ref,
    source, vertical, north, east,
    z_phi, z_psi, z_first, z_second,
    y_rate, y_phi, y_psi, y_first, y_second, y_value, y_part,
    x_phi, x_psi, x_phi2, x_psi2, x_first, x_second, x_first2, x_second2,
    x_part, x_part2, plane, hold,
    y_coef, y_ends, y_ends2, x_coef, x_coef_in, x_ends, x_ends_in, x_back, x_back_in,
    y_fac, y_scan, x_fac,
    load_sem, send_sem, recv_sem,
):
    lines = nx * nz
    blocks = lines // LANES
    pl_me, xs_me = lax.axis_index("pl"), lax.axis_index("xs")

    side, chips, half = math.isqrt(n_pl), n_xs // 2, n_xs // 2
    pl_row, pl_col = pl_me // side, lax.rem(pl_me, side)
    chip, core = xs_me // 2, lax.rem(xs_me, 2)
    pair = lax.rem(xs_me, half)

    def ring(offset, count):
        return min(offset, count - offset)

    steps = [(r, c) for r in range(side) for c in range(side) if r or c]
    steps.sort(key=lambda step: -ring(step[0], side) - ring(step[1], side))
    pl_peers = [lax.rem(pl_row + r, side) * side + lax.rem(pl_col + c, side) for r, c in steps]
    xs_offsets = sorted(range(1, n_xs), key=lambda offset: -ring(offset, n_xs))
    xs_peers = [lax.rem(xs_me + offset, n_xs) for offset in xs_offsets]
    near = sorted(range(-(chips // 8), chips // 2 - chips // 8), key=lambda offset: -abs(offset))
    near_peers = [lax.rem(chip + offset + chips, chips) * 2 + c for offset in near if offset for c in range(2)]
    near_peers.append(xs_me + 1 - 2 * core)

    barrier = pltpu.get_barrier_semaphore()
    for axis, peers in (("xs", xs_peers), ("pl", pl_peers)):
        for peer in peers:
            pl.semaphore_signal(barrier, 1, device_id={axis: peer}, device_id_type=MESH)

    loads = []
    for slot, (hbm, vmem) in enumerate(
        ((north_hbm, north), (vertical_hbm, vertical), (source_hbm, source), (east_hbm, east))
    ):
        copy = pltpu.make_async_copy(hbm, vmem, load_sem.at[slot])
        copy.start()
        loads.append(copy)

    def share(axis, slot, peers, pick, landing, place):
        for peer in peers:
            pltpu.make_async_remote_copy(
                src_ref=pick(peer),
                dst_ref=landing.at[place],
                send_sem=send_sem.at[slot],
                recv_sem=recv_sem.at[slot],
                device_id={axis: peer},
                device_id_type=MESH,
            ).start()

    def arrived(slot, landing, sem=None):
        count = landing.shape[0]
        if count > 1:
            whole = landing.at[pl.ds(0, count - 1)]
            sem = recv_sem if sem is None else sem
            pltpu.make_async_copy(whole, whole, sem.at[slot]).wait()

    def rows(b):
        return pl.ds(b * LANES, LANES)

    def across(y):
        return pl.ds(y, blocks, stride=LANES)

    loads[0].wait()
    for b in range(blocks):
        y_rate[rows(b)] = (1.0 / north[rows(b)]).T

    def y_sweep(i, carry):
        phi, phi_step, psi, psi_step = carry
        y_phi[across(i)] = phi
        y_psi[across(LANES - 1 - i)] = psi
        phi_step = phi_step + phi * y_rate[across(i)]
        psi_step = psi_step + psi * y_rate[across(LANES - 1 - i)]
        return phi + phi_step, phi_step, psi + psi_step, psi_step

    unit = jnp.ones((blocks, LANES), jnp.float32)
    y_phi_end = lax.fori_loop(0, LANES, y_sweep, (unit, unit, unit, unit), unroll=8)[0]
    y_inv = 1.0 / y_phi_end
    hold[pl.ds(0, blocks)] = y_inv
    for b in range(blocks):
        inv = hold[b:b + 1]
        scaled = y_rate[rows(b)] * inv
        y_first[rows(b)] = y_phi[rows(b)] * scaled
        y_second[rows(b)] = y_psi[rows(b)] * scaled
    y_coef[pl_me, 0] = y_psi[across(0)] * y_inv
    y_coef[pl_me, 1] = y_phi[across(LANES - 1)] * y_inv
    y_coef[pl_me, 2] = y_inv

    pl.semaphore_wait(barrier, n_pl + n_xs - 2)
    share("pl", 0, pl_peers, lambda peer: y_coef.at[pl_me], y_coef, pl_me)

    def level(z):
        return pl.ds(z, nx, stride=nz)

    loads[1].wait()
    phi = jnp.ones((nx, LANES), jnp.float32)
    phi_step = psi = psi_step = phi
    for z in range(nz):
        back = nz - 1 - z
        up, down = 1.0 / vertical[level(z)], 1.0 / vertical[level(back)]
        z_phi[z] = phi
        z_psi[back] = psi
        z_first[z] = phi * up
        z_second[back] = psi * down
        phi_step = phi_step + phi * up
        psi_step = psi_step + psi * down
        phi = phi + phi_step
        psi = psi + psi_step
    z_inv = 1.0 / phi
    for z in range(nz):
        z_first[z] = z_first[z] * z_inv
        z_second[z] = z_second[z] * z_inv

    def z_solve(read, write):
        def keep(z, value=None):
            if value is None:
                return x_part2[pl.ds(z * nx, nx)]
            x_part2[pl.ds(z * nx, nx)] = value

        running(nz, lambda z: z_first[z], lambda z: z_second[z], read, lambda z: z_phi[z], lambda z: z_psi[z], keep, write)

    loads[2].wait()

    def to_plane(z, value):
        plane[level(z)] = value

    z_solve(lambda z: source[level(z)], to_plane)

    low = lax.broadcasted_iota(jnp.int32, (LANES, LANES), 0)
    high = lax.broadcasted_iota(jnp.int32, (LANES, LANES), 1)
    upto = jnp.where(high <= low, 1.0, 0.0)
    beyond = jnp.where(high > low, 1.0, 0.0)

    def y_send(slot, ends):
        for b in range(blocks):
            value = plane[rows(b)].T
            second = y_second[rows(b)] * value
            first = y_first[rows(b)] * value
            y_value[rows(b)] = first
            y_part[rows(b)] = second
            ends[pl_me, 0, b:b + 1] = jnp.sum(second, axis=0, keepdims=True)
            ends[pl_me, 1, b:b + 1] = jnp.sum(first, axis=0, keepdims=True)
        share("pl", slot, pl_peers, lambda peer: ends.at[pl_me], ends, pl_me)

    def y_local():
        for b in range(blocks):
            below = jnp.dot(upto, y_value[rows(b)], precision=HIGHEST, preferred_element_type=jnp.float32)
            above = jnp.dot(beyond, y_part[rows(b)], precision=HIGHEST, preferred_element_type=jnp.float32)
            y_part[rows(b)] = y_psi[rows(b)] * below + y_phi[rows(b)] * above

    def y_finish(slot, ends):
        arrived(slot, ends)
        a = c = jnp.zeros((blocks, LANES), jnp.float32)
        y_scan[0, 0] = a
        y_scan[1, n_pl] = c
        for j in range(n_pl):
            k = n_pl - 1 - j
            a = ends[j, 1] + y_fac[2, j] * ends[j, 0] + y_fac[1, j] * a
            c = ends[k, 0] + y_fac[4, k] * ends[k, 1] + y_fac[3, k] * c
            y_scan[0, j + 1] = a
            y_scan[1, k] = c
        a_here, a_next = y_scan[0, pl_me], y_scan[0, pl_me + 1]
        c_here, c_next = y_scan[1, pl_me], y_scan[1, pl_me + 1]
        outside_low = (a_here + y_fac[0, pl_me] * c_here) * y_fac[6, pl_me]
        outside_high = (c_next + y_fac[5, pl_me + 1] * a_next) * y_fac[6, pl_me + 1]
        inv = y_coef[pl_me, 2]
        hold[pl.ds(0, blocks)] = outside_low * inv
        hold[pl.ds(blocks, blocks)] = outside_high * inv
        for b in range(blocks):
            solved = (
                y_part[rows(b)]
                + y_psi[rows(b)] * hold[b:b + 1]
                + y_phi[rows(b)] * hold[blocks + b:blocks + b + 1]
            )
            plane[rows(b)] = solved.T

    y_send(1, y_ends)

    def step(i):
        return pl.ds(i * nz, nz)

    loads[3].wait()
    phi = jnp.ones((nz, LANES), jnp.float32)
    phi_step = psi = psi_step = phi
    for i in range(nx):
        back = nx - 1 - i
        up, down = 1.0 / east[step(i)], 1.0 / east[step(back)]
        x_phi[step(i)] = phi
        x_psi[step(back)] = psi
        x_first[step(i)] = phi * up
        x_second[step(back)] = psi * down
        phi_step = phi_step + phi * up
        psi_step = psi_step + psi * down
        phi = phi + phi_step
        psi = psi + psi_step
    x_inv = 1.0 / phi
    for i in range(nx):
        x_first[step(i)] = x_first[step(i)] * x_inv
        x_second[step(i)] = x_second[step(i)] * x_inv

    def x_solve(read, write):
        def keep(i, value=None):
            if value is None:
                return x_part2[step(i)]
            x_part2[step(i)] = value

        running(
            nx, lambda i: x_first[step(i)], lambda i: x_second[step(i)], read,
            lambda i: x_phi[step(i)], lambda i: x_psi[step(i)], keep, write,
        )

    def into(ref):
        def write(i, value):
            ref[step(i)] = value

        return write

    x_solve(lambda i: x_phi[step(i)], into(x_phi2))
    x_solve(lambda i: x_psi[step(i)], into(x_psi2))
    for i in range(nx):
        scaled = x_inv * (1.0 / east[step(i)])
        x_first2[step(i)] = x_phi2[step(i)] * scaled
        x_second2[step(i)] = x_psi2[step(i)] * scaled
    last = step(nx - 1)
    def halves(ref, quantity, value):
        group, at = quantity
        for k in range(2):
            ref[(slice(None),) + group + (at + k,)] = value[k * half:(k + 1) * half]

    coefficients = (
        x_psi[step(0)], x_phi[last], None, x_psi2[step(0)], x_phi2[last], x_phi2[step(0)],
    )
    for q, value in enumerate(coefficients):
        halves(x_coef, ((q // 2,), q % 2 * 2), x_inv if value is None else value * x_inv)
    share("xs", 2, xs_peers, lambda peer: x_coef.at[lax.rem(peer, half)], x_coef_in, xs_me)
    x_coef_in[xs_me] = x_coef[pair]

    names = {"b": 0, "a1": 1, "a2": 2, "c1": 3, "c2": 4, "d": 5, "g": 6}
    arrived(0, y_coef)

    def y_store(name, j, value):
        y_fac[names[name], j] = value

    reduced_factors(n_pl, lambda j: (y_coef[j, 0], y_coef[j, 1], y_coef[j, 2]), y_store)
    y_local()
    y_finish(1, y_ends)

    p0 = pn = q0 = qn = jnp.zeros((nz, LANES), jnp.float32)
    for i in range(nx):
        value = plane[step(i)]
        p0 = p0 + x_second[step(i)] * value
        pn = pn + x_first[step(i)] * value
        q0 = q0 + x_second2[step(i)] * value
        qn = qn + x_first2[step(i)] * value
    for q, value in enumerate((p0, pn, q0, qn)):
        halves(x_ends, ((), 2 * q), value)
    share("xs", 3, xs_peers, lambda peer: x_ends.at[lax.rem(peer, half)], x_ends_in, xs_me)
    x_ends_in[xs_me] = x_ends[pair]

    arrived(2, x_coef_in)

    def x_store(name, j, value):
        x_fac[names[name], j] = value

    def coef(j, q):
        return x_coef_in[j, q // 2, q % 2 * 2:q % 2 * 2 + 2]

    reduced_factors(n_xs, lambda j: (coef(j, 0), coef(j, 1), coef(j, 2)), x_store)
    x_solve(lambda i: plane[step(i)], into(x_part))

    arrived(3, x_ends_in)

    def fac(name, j):
        return x_fac[names[name], j]

    def x_reduced(ends):
        a = c = jnp.zeros((2, LANES), jnp.float32)
        lefts, rights = [a], [c]
        for j in range(n_xs):
            k = n_xs - 1 - j
            a = ends[j][1] + fac("a2", j) * ends[j][0] + fac("a1", j) * a
            c = ends[k][0] + fac("c2", k) * ends[k][1] + fac("c1", k) * c
            lefts.append(a)
            rights.append(c)
        rights = rights[::-1]
        lows = [(lefts[j] + fac("b", j) * rights[j]) * fac("g", j) for j in range(n_xs)]
        highs = [
            (rights[j + 1] + fac("d", j + 1) * lefts[j + 1]) * fac("g", j + 1) for j in range(n_xs)
        ]
        return lows, highs

    def end(j, q):
        return x_ends_in[j, 2 * q:2 * q + 2]

    lows, highs = x_reduced([(end(j, 0), end(j, 1)) for j in range(n_xs)])
    again = []
    for j in range(n_xs):
        left, right, shared = coef(j, 3), coef(j, 4), coef(j, 5)
        again.append(
            (
                end(j, 2) + left * lows[j] + shared * highs[j],
                end(j, 3) + shared * lows[j] + right * highs[j],
            )
        )
    lows2, highs2 = x_reduced(again)
    for j in range(n_xs):
        for q, value in enumerate((lows[j], highs[j], lows2[j], highs2[j])):
            x_back[j, 2 * q:2 * q + 2] = value * coef(j, 2)
    share("xs", 4, near_peers, lambda peer: x_back.at[peer], x_back_in, pair)
    x_back_in[pair] = x_back[xs_me]

    x_solve(lambda i: x_part[step(i)], into(x_part))
    arrived(4, x_back_in)
    low1, high1, low2, high2 = (
        jnp.concatenate([x_back_in[:, 2 * q], x_back_in[:, 2 * q + 1]], axis=0) for q in range(4)
    )
    for i in range(nx):
        plane[step(i)] = (
            x_part[step(i)]
            + x_psi2[step(i)] * low1
            + x_phi2[step(i)] * high1
            + x_psi[step(i)] * low2
            + x_phi[step(i)] * high2
        )

    y_send(5, y_ends2)
    y_local()
    y_finish(5, y_ends2)

    def to_out(z, value):
        out_ref[level(z)] = value

    z_solve(lambda z: plane[level(z)], to_out)

    arrived(0, y_coef, send_sem)
    arrived(1, y_ends, send_sem)
    arrived(2, x_coef_in, send_sem)
    arrived(3, x_ends_in, send_sem)
    arrived(4, x_back_in, send_sem)
    arrived(5, y_ends2, send_sem)


def shards(n_pl, n_xs, source, eastward_rate, northward_rate, vertical_rate, amplitude):
    nx, nz, ny = source.shape
    lines = nx * nz
    blocks = lines // LANES
    flat = lambda array: pltpu.with_memory_space_constraint(array.reshape(lines, ny), pltpu.HBM)
    field = pltpu.VMEM((lines, LANES), jnp.float32)
    column = pltpu.VMEM((nz, nx, LANES), jnp.float32)
    vmem = lambda *shape: pltpu.VMEM(shape, jnp.float32)
    second = pl.pallas_call(
        functools.partial(kernel, nx, nz, n_pl, n_xs),
        out_shape=jax.ShapeDtypeStruct((lines, ny), jnp.float32),
        in_specs=[pl.BlockSpec(memory_space=pltpu.HBM)] * 4,
        out_specs=pl.BlockSpec(memory_space=pltpu.VMEM),
        scratch_shapes=[field] * 4
        + [column] * 4
        + [field] * 7
        + [field] * 8
        + [field] * 3
        + [vmem(2 * blocks, LANES)]
        + [
            vmem(n_pl, 3, blocks, LANES),
            vmem(n_pl, 2, blocks, LANES),
            vmem(n_pl, 2, blocks, LANES),
            vmem(n_xs // 2, 3, 4, LANES),
            vmem(n_xs, 3, 4, LANES),
            vmem(n_xs // 2, 8, LANES),
            vmem(n_xs, 8, LANES),
            vmem(n_xs, 8, LANES),
            vmem(n_xs // 2, 8, LANES),
            vmem(7, n_pl + 1, blocks, LANES),
            vmem(2, n_pl + 1, blocks, LANES),
            vmem(7, n_xs + 1, 2, LANES),
            pltpu.SemaphoreType.DMA((4,)),
            pltpu.SemaphoreType.DMA((6,)),
            pltpu.SemaphoreType.DMA((6,)),
        ],
        compiler_params=pltpu.CompilerParams(
            collective_id=0, has_side_effects=True, vmem_limit_bytes=40 * 1024 * 1024
        ),
        name="adi",
    )(flat(source), flat(vertical_rate), flat(northward_rate), flat(eastward_rate))
    return amplitude * second.reshape(nx, nz, ny)


def solution(mesh):
    spec = P("xs", None, "pl")
    return jax.shard_map(
        functools.partial(shards, mesh.shape["pl"], mesh.shape["xs"]),
        mesh=mesh,
        in_specs=(spec,) * 5,
        out_specs=spec,
        check_vma=False,
    )
```

```python
import functools
import math

import jax
import jax.numpy as jnp
from jax import lax
from jax.experimental import pallas as pl
from jax.experimental.pallas import tpu as pltpu
from jax.sharding import PartitionSpec as P

MESH = pl.DeviceIdType.MESH
LANES = 128
HIGHEST = lax.Precision.HIGHEST


def reduced_factors(count, load, store):
    one = None
    b = None
    forward = []
    for j in range(count):
        left, right, shared = load(j)
        if b is None:
            b = jnp.zeros_like(left)
            one = jnp.ones_like(left)
        store("b", j, b)
        a1 = shared / (one - left * b)
        a2 = a1 * b
        store("a1", j, a1)
        store("a2", j, a2)
        b = right + a2 * shared
        forward.append(b)
    store("b", count, b)
    d = jnp.zeros_like(b)
    store("d", count, d)
    store("g", count, one)
    for j in reversed(range(count)):
        left, right, shared = load(j)
        c1 = shared / (one - right * d)
        c2 = c1 * d
        store("c1", j, c1)
        store("c2", j, c2)
        d = left + c2 * shared
        store("d", j, d)
        before = forward[j - 1] if j else jnp.zeros_like(d)
        store("g", j, one / (one - before * d))


def running(count, first, second, value, phi, psi, keep, emit):
    total = None
    for i in reversed(range(count)):
        term = second(i) * value(i)
        if total is None:
            total = jnp.zeros_like(term)
        keep(i, total)
        total = total + term
    total = jnp.zeros_like(total)
    for i in range(count):
        total = total + first(i) * value(i)
        emit(i, psi(i) * total + phi(i) * keep(i))


def kernel(
    nx, nz, n_pl, n_xs,
    source_hbm, vertical_hbm, north_hbm, east_hbm, out_ref,
    source, vertical, north, east,
    z_phi, z_psi, z_first, z_second,
    y_rate, y_phi, y_psi, y_first, y_second, y_value, y_part,
    x_phi, x_psi, x_phi2, x_psi2, x_first, x_second, x_first2, x_second2,
    x_part, x_part2, plane, hold,
    y_coef, y_ends, y_ends2, x_coef, x_two_coef, x_chip_coef, x_ends, x_two, x_chip,
    x_outside, x_back, x_back_in, x_meet, y_fac, y_scan, x_fac,
    load_sem, send_sem, recv_sem,
):
    lines = nx * nz
    blocks = lines // LANES
    pl_me, xs_me = lax.axis_index("pl"), lax.axis_index("xs")

    side, chips, half = math.isqrt(n_pl), n_xs // 2, nz // 2
    pl_row, pl_col = pl_me // side, lax.rem(pl_me, side)
    chip, core = xs_me // 2, lax.rem(xs_me, 2)
    other = 1 - core

    def ring(offset, count):
        return min(offset, count - offset)

    steps = [(r, c) for r in range(side) for c in range(side) if r or c]
    steps.sort(key=lambda step: -ring(step[0], side) - ring(step[1], side))
    pl_peers = [lax.rem(pl_row + r, side) * side + lax.rem(pl_col + c, side) for r, c in steps]
    ring_offsets = sorted(range(1, chips), key=lambda offset: -ring(offset, chips))
    ring_peers = [lax.rem(chip + offset, chips) * 2 + core for offset in ring_offsets]
    mate = [chip * 2 + other]

    barrier = pltpu.get_barrier_semaphore()
    for axis, peers in (("pl", pl_peers), ("xs", ring_peers + mate)):
        for peer in peers:
            pl.semaphore_signal(barrier, 1, device_id={axis: peer}, device_id_type=MESH)

    loads = []
    for slot, (hbm, vmem) in enumerate(
        ((north_hbm, north), (vertical_hbm, vertical), (source_hbm, source), (east_hbm, east))
    ):
        copy = pltpu.make_async_copy(hbm, vmem, load_sem.at[slot])
        copy.start()
        loads.append(copy)

    def share(axis, slot, peers, source_ref, landing_ref):
        for peer in peers:
            pltpu.make_async_remote_copy(
                src_ref=source_ref,
                dst_ref=landing_ref,
                send_sem=send_sem.at[slot],
                recv_sem=recv_sem.at[slot],
                device_id={axis: peer},
                device_id_type=MESH,
            ).start()

    def arrived(slot, landing, sem=None):
        sem = recv_sem if sem is None else sem
        pltpu.make_async_copy(landing, landing, sem.at[slot]).wait()

    def others(landing):
        return landing.at[pl.ds(0, landing.shape[0] - 1)]

    def rows(b):
        return pl.ds(b * LANES, LANES)

    def across(y):
        return pl.ds(y, blocks, stride=LANES)

    loads[0].wait()
    for b in range(blocks):
        y_rate[rows(b)] = (1.0 / north[rows(b)]).T

    def y_sweep(i, carry):
        phi, phi_step, psi, psi_step = carry
        y_phi[across(i)] = phi
        y_psi[across(LANES - 1 - i)] = psi
        phi_step = phi_step + phi * y_rate[across(i)]
        psi_step = psi_step + psi * y_rate[across(LANES - 1 - i)]
        return phi + phi_step, phi_step, psi + psi_step, psi_step

    unit = jnp.ones((blocks, LANES), jnp.float32)
    y_phi_end = lax.fori_loop(0, LANES, y_sweep, (unit, unit, unit, unit), unroll=8)[0]
    y_inv = 1.0 / y_phi_end
    hold[pl.ds(0, blocks)] = y_inv
    for b in range(blocks):
        inv = hold[b:b + 1]
        scaled = y_rate[rows(b)] * inv
        y_first[rows(b)] = y_phi[rows(b)] * scaled
        y_second[rows(b)] = y_psi[rows(b)] * scaled
    y_coef[pl_me, 0] = y_psi[across(0)] * y_inv
    y_coef[pl_me, 1] = y_phi[across(LANES - 1)] * y_inv
    y_coef[pl_me, 2] = y_inv

    pl.semaphore_wait(barrier, n_pl + chips - 1)
    share("pl", 0, pl_peers, y_coef.at[pl_me], y_coef.at[pl_me])

    def level(z):
        return pl.ds(z, nx, stride=nz)

    loads[1].wait()
    phi = jnp.ones((nx, LANES), jnp.float32)
    phi_step = psi = psi_step = phi
    for z in range(nz):
        back = nz - 1 - z
        up, down = 1.0 / vertical[level(z)], 1.0 / vertical[level(back)]
        z_phi[z] = phi
        z_psi[back] = psi
        z_first[z] = phi * up
        z_second[back] = psi * down
        phi_step = phi_step + phi * up
        psi_step = psi_step + psi * down
        phi = phi + phi_step
        psi = psi + psi_step
    z_inv = 1.0 / phi
    for z in range(nz):
        z_first[z] = z_first[z] * z_inv
        z_second[z] = z_second[z] * z_inv

    def z_solve(read, write):
        def keep(z, value=None):
            if value is None:
                return x_part2[pl.ds(z * nx, nx)]
            x_part2[pl.ds(z * nx, nx)] = value

        running(nz, lambda z: z_first[z], lambda z: z_second[z], read, lambda z: z_phi[z], lambda z: z_psi[z], keep, write)

    loads[2].wait()

    def to_plane(z, value):
        plane[level(z)] = value

    z_solve(lambda z: source[level(z)], to_plane)

    low = lax.broadcasted_iota(jnp.int32, (LANES, LANES), 0)
    high = lax.broadcasted_iota(jnp.int32, (LANES, LANES), 1)
    upto = jnp.where(high <= low, 1.0, 0.0)
    beyond = jnp.where(high > low, 1.0, 0.0)

    def y_send(slot, ends):
        for b in range(blocks):
            value = plane[rows(b)].T
            second = y_second[rows(b)] * value
            first = y_first[rows(b)] * value
            y_value[rows(b)] = first
            y_part[rows(b)] = second
            ends[pl_me, 0, b:b + 1] = jnp.sum(second, axis=0, keepdims=True)
            ends[pl_me, 1, b:b + 1] = jnp.sum(first, axis=0, keepdims=True)
        share("pl", slot, pl_peers, ends.at[pl_me], ends.at[pl_me])

    def y_local():
        for b in range(blocks):
            below = jnp.dot(upto, y_value[rows(b)], precision=HIGHEST, preferred_element_type=jnp.float32)
            above = jnp.dot(beyond, y_part[rows(b)], precision=HIGHEST, preferred_element_type=jnp.float32)
            y_part[rows(b)] = y_psi[rows(b)] * below + y_phi[rows(b)] * above

    def y_finish(slot, ends):
        arrived(slot, others(ends))
        a = c = jnp.zeros((blocks, LANES), jnp.float32)
        y_scan[0, 0] = a
        y_scan[1, n_pl] = c
        for j in range(n_pl):
            k = n_pl - 1 - j
            a = ends[j, 1] + y_fac[2, j] * ends[j, 0] + y_fac[1, j] * a
            c = ends[k, 0] + y_fac[4, k] * ends[k, 1] + y_fac[3, k] * c
            y_scan[0, j + 1] = a
            y_scan[1, k] = c
        a_here, a_next = y_scan[0, pl_me], y_scan[0, pl_me + 1]
        c_here, c_next = y_scan[1, pl_me], y_scan[1, pl_me + 1]
        outside_low = (a_here + y_fac[0, pl_me] * c_here) * y_fac[6, pl_me]
        outside_high = (c_next + y_fac[5, pl_me + 1] * a_next) * y_fac[6, pl_me + 1]
        inv = y_coef[pl_me, 2]
        hold[pl.ds(0, blocks)] = outside_low * inv
        hold[pl.ds(blocks, blocks)] = outside_high * inv
        for b in range(blocks):
            solved = (
                y_part[rows(b)]
                + y_psi[rows(b)] * hold[b:b + 1]
                + y_phi[rows(b)] * hold[blocks + b:blocks + b + 1]
            )
            plane[rows(b)] = solved.T

    y_send(1, y_ends)

    def step(i):
        return pl.ds(i * nz, nz)

    loads[3].wait()
    phi = jnp.ones((nz, LANES), jnp.float32)
    phi_step = psi = psi_step = phi
    for i in range(nx):
        back = nx - 1 - i
        up, down = 1.0 / east[step(i)], 1.0 / east[step(back)]
        x_phi[step(i)] = phi
        x_psi[step(back)] = psi
        x_first[step(i)] = phi * up
        x_second[step(back)] = psi * down
        phi_step = phi_step + phi * up
        psi_step = psi_step + psi * down
        phi = phi + phi_step
        psi = psi + psi_step
    x_inv = 1.0 / phi
    for i in range(nx):
        x_first[step(i)] = x_first[step(i)] * x_inv
        x_second[step(i)] = x_second[step(i)] * x_inv

    def x_solve(read, write):
        def keep(i, value=None):
            if value is None:
                return x_part2[step(i)]
            x_part2[step(i)] = value

        running(
            nx, lambda i: x_first[step(i)], lambda i: x_second[step(i)], read,
            lambda i: x_phi[step(i)], lambda i: x_psi[step(i)], keep, write,
        )

    def into(ref):
        def write(i, value):
            ref[step(i)] = value

        return write

    x_solve(lambda i: x_phi[step(i)], into(x_phi2))
    x_solve(lambda i: x_psi[step(i)], into(x_psi2))
    for i in range(nx):
        scaled = x_inv * (1.0 / east[step(i)])
        x_first2[step(i)] = x_phi2[step(i)] * scaled
        x_second2[step(i)] = x_psi2[step(i)] * scaled
    last = step(nx - 1)
    coefficients = (
        x_psi[step(0)] * x_inv, x_phi[last] * x_inv, x_inv,
        x_psi2[step(0)] * x_inv, x_phi2[last] * x_inv, x_phi2[step(0)] * x_inv,
    )
    for q, value in enumerate(coefficients):
        x_coef[0, q] = value[:half]
        x_coef[1, q] = value[half:]
    x_two_coef[core] = x_coef[core]
    share("xs", 2, mate, x_coef.at[other], x_two_coef.at[core])

    y_local()

    arrived(2, x_two_coef.at[0])
    left_a, right_a, shared_a, left2_a, right2_a, shared2_a = (x_two_coef[0, q] for q in range(6))
    left_b, right_b, shared_b, left2_b, right2_b, shared2_b = (x_two_coef[1, q] for q in range(6))
    meet = 1.0 / (1.0 - right_a * left_b)
    last_low, last_high = meet * shared_a, meet * right_a * shared_b
    first_low, first_high = meet * left_b * shared_a, meet * shared_b
    x_meet[0] = meet
    for q, value in enumerate((last_low, last_high, first_low, first_high)):
        x_meet[q + 1] = value

    def joined(p0a, pna, p0b, pnb):
        return (
            p0a + shared_a * (meet * (p0b + left_b * pna)),
            pnb + shared_b * (meet * (pna + right_a * p0b)),
        )

    first_from_low, _ = joined(
        left2_a + shared2_a * first_low, shared2_a + right2_a * first_low,
        left2_b * last_low, shared2_b * last_low,
    )
    first_from_high, last_from_high = joined(
        shared2_a * first_high, right2_a * first_high,
        left2_b * last_high + shared2_b, shared2_b * last_high + right2_b,
    )
    merged = (
        left_a + shared_a * first_low, right_b + shared_b * last_high, shared_a * first_high,
        first_from_low, last_from_high, first_from_high,
    )
    for q, value in enumerate(merged):
        x_chip_coef[chip, q] = value
    share("xs", 3, ring_peers, x_chip_coef.at[chip], x_chip_coef.at[chip])

    names = {"b": 0, "a1": 1, "a2": 2, "c1": 3, "c2": 4, "d": 5, "g": 6}
    arrived(0, others(y_coef))

    def y_store(name, j, value):
        y_fac[names[name], j] = value

    reduced_factors(n_pl, lambda j: (y_coef[j, 0], y_coef[j, 1], y_coef[j, 2]), y_store)
    y_finish(1, y_ends)

    p0 = pn = q0 = qn = jnp.zeros((nz, LANES), jnp.float32)
    for i in range(nx):
        value = plane[step(i)]
        p0 = p0 + x_second[step(i)] * value
        pn = pn + x_first[step(i)] * value
        q0 = q0 + x_second2[step(i)] * value
        qn = qn + x_first2[step(i)] * value
    for q, value in enumerate((p0, pn, q0, qn)):
        x_ends[0, q] = value[:half]
        x_ends[1, q] = value[half:]
    share("xs", 4, mate, x_ends.at[other], x_two.at[core])
    x_two[core] = x_ends[core]

    x_solve(lambda i: plane[step(i)], into(x_part))

    arrived(4, x_two.at[0])
    left_a, right_a, shared_a, left2_a, right2_a, shared2_a = (x_two_coef[0, q] for q in range(6))
    left_b, right_b, shared_b, left2_b, right2_b, shared2_b = (x_two_coef[1, q] for q in range(6))
    meet, last_low, last_high, first_low, first_high = (x_meet[q] for q in range(5))

    def border(p0b, pna):
        return meet * (pna + right_a * p0b), meet * (p0b + left_b * pna)

    def ends_again(last_a, first_b, low, high):
        p0a, pna = x_two[0, 2] + shared2_a * first_b, x_two[0, 3] + right2_a * first_b
        p0b, pnb = x_two[1, 2] + left2_b * last_a, x_two[1, 3] + shared2_b * last_a
        if low is not None:
            p0a, pna = p0a + left2_a * low, pna + shared2_a * low
            p0b, pnb = p0b + shared2_b * high, pnb + right2_b * high
        return p0a, pna, p0b, pnb

    last_a, first_b = border(x_two[1, 0], x_two[0, 1])
    x_chip[chip, 0] = x_two[0, 0] + shared_a * first_b
    x_chip[chip, 1] = x_two[1, 1] + shared_b * last_a
    p0a, pna, p0b, pnb = ends_again(last_a, first_b, None, None)
    last2, first2 = border(p0b, pna)
    x_chip[chip, 2] = p0a + shared_a * first2
    x_chip[chip, 3] = pnb + shared_b * last2
    share("xs", 5, ring_peers, x_chip.at[chip], x_chip.at[chip])

    arrived(3, others(x_chip_coef))

    def x_store(name, j, value):
        x_fac[names[name], j] = value

    reduced_factors(
        chips, lambda j: (x_chip_coef[j, 0], x_chip_coef[j, 1], x_chip_coef[j, 2]), x_store
    )
    x_solve(lambda i: x_part[step(i)], into(x_part))

    arrived(5, others(x_chip))

    def fac(name, j):
        return x_fac[names[name], j]

    def x_reduced(ends):
        a = c = jnp.zeros((half, LANES), jnp.float32)
        lefts, rights = [a], [c]
        for j in range(chips):
            k = chips - 1 - j
            a = ends[j][1] + fac("a2", j) * ends[j][0] + fac("a1", j) * a
            c = ends[k][0] + fac("c2", k) * ends[k][1] + fac("c1", k) * c
            lefts.append(a)
            rights.append(c)
        rights = rights[::-1]
        lows = [(lefts[j] + fac("b", j) * rights[j]) * fac("g", j) for j in range(chips)]
        highs = [
            (rights[j + 1] + fac("d", j + 1) * lefts[j + 1]) * fac("g", j + 1) for j in range(chips)
        ]
        return lows, highs

    lows, highs = x_reduced([(x_chip[j, 0], x_chip[j, 1]) for j in range(chips)])
    again = []
    for j in range(chips):
        left, right, shared = (x_chip_coef[j, q] for q in range(3, 6))
        again.append(
            (
                x_chip[j, 2] + left * lows[j] + shared * highs[j],
                x_chip[j, 3] + shared * lows[j] + right * highs[j],
            )
        )
    lows2, highs2 = x_reduced(again)
    for j in range(chips):
        for q, value in enumerate((lows[j], highs[j], lows2[j], highs2[j])):
            x_outside[j, q] = value
    low, high, low2, high2 = (x_outside[chip, q] for q in range(4))
    last_a, first_b = border(x_two[1, 0], x_two[0, 1])
    last_a = last_a + last_low * low + last_high * high
    first_b = first_b + first_low * low + first_high * high
    p0a, pna, p0b, pnb = ends_again(last_a, first_b, low, high)
    last2, first2 = border(p0b, pna)
    last2 = last2 + last_low * low2 + last_high * high2
    first2 = first2 + first_low * low2 + first_high * high2
    for q, value in enumerate((low, first_b, low2, first2)):
        x_back[0, q] = value
    for q, value in enumerate((last_a, high, last2, high2)):
        x_back[1, q] = value
    share("xs", 6, mate, x_back.at[other], x_back_in.at[core])
    x_back_in[core] = x_back[core]

    arrived(6, x_back_in.at[0])
    low1, high1, low2, high2 = (
        jnp.concatenate([x_back_in[0, q], x_back_in[1, q]], axis=0) * x_inv for q in range(4)
    )
    for i in range(nx):
        plane[step(i)] = (
            x_part[step(i)]
            + x_psi2[step(i)] * low1
            + x_phi2[step(i)] * high1
            + x_psi[step(i)] * low2
            + x_phi[step(i)] * high2
        )

    y_send(7, y_ends2)
    y_local()
    y_finish(7, y_ends2)

    def to_out(z, value):
        out_ref[level(z)] = value

    z_solve(lambda z: plane[level(z)], to_out)

    for slot, landing in enumerate(
        (
            others(y_coef), others(y_ends), x_two_coef.at[0], others(x_chip_coef),
            x_two.at[0], others(x_chip), x_back_in.at[0], others(y_ends2),
        )
    ):
        arrived(slot, landing, send_sem)


def shards(n_pl, n_xs, source, eastward_rate, northward_rate, vertical_rate, amplitude):
    nx, nz, ny = source.shape
    lines = nx * nz
    blocks = lines // LANES
    chips, half = n_xs // 2, nz // 2
    flat = lambda array: pltpu.with_memory_space_constraint(array.reshape(lines, ny), pltpu.HBM)
    field = pltpu.VMEM((lines, LANES), jnp.float32)
    column = pltpu.VMEM((nz, nx, LANES), jnp.float32)
    vmem = lambda *shape: pltpu.VMEM(shape, jnp.float32)
    second = pl.pallas_call(
        functools.partial(kernel, nx, nz, n_pl, n_xs),
        out_shape=jax.ShapeDtypeStruct((lines, ny), jnp.float32),
        in_specs=[pl.BlockSpec(memory_space=pltpu.HBM)] * 4,
        out_specs=pl.BlockSpec(memory_space=pltpu.VMEM),
        scratch_shapes=[field] * 4
        + [column] * 4
        + [field] * 7
        + [field] * 8
        + [field] * 3
        + [vmem(2 * blocks, LANES)]
        + [
            vmem(n_pl, 3, blocks, LANES),
            vmem(n_pl, 2, blocks, LANES),
            vmem(n_pl, 2, blocks, LANES),
            vmem(2, 6, half, LANES),
            vmem(2, 6, half, LANES),
            vmem(chips, 6, half, LANES),
            vmem(2, 4, half, LANES),
            vmem(2, 4, half, LANES),
            vmem(chips, 4, half, LANES),
            vmem(chips, 4, half, LANES),
            vmem(2, 4, half, LANES),
            vmem(2, 4, half, LANES),
            vmem(5, half, LANES),
            vmem(7, n_pl + 1, blocks, LANES),
            vmem(2, n_pl + 1, blocks, LANES),
            vmem(7, chips + 1, half, LANES),
            pltpu.SemaphoreType.DMA((4,)),
            pltpu.SemaphoreType.DMA((8,)),
            pltpu.SemaphoreType.DMA((8,)),
        ],
        compiler_params=pltpu.CompilerParams(
            collective_id=0, has_side_effects=True, vmem_limit_bytes=40 * 1024 * 1024
        ),
        name="adi",
    )(flat(source), flat(vertical_rate), flat(northward_rate), flat(eastward_rate))
    return amplitude * second.reshape(nx, nz, ny)


def solution(mesh):
    spec = P("xs", None, "pl")
    return jax.shard_map(
        functools.partial(shards, mesh.shape["pl"], mesh.shape["xs"]),
        mesh=mesh,
        in_specs=(spec,) * 5,
        out_specs=spec,
        check_vma=False,
    )
```

```python
import functools
import math

import jax
import jax.numpy as jnp
from jax import lax
from jax.experimental import pallas as pl
from jax.experimental.pallas import tpu as pltpu
from jax.sharding import PartitionSpec as P

MESH = pl.DeviceIdType.MESH
LANES = 128
Y_PITCH = LANES + 8
Z_SPARE = 8
HIGHEST = lax.Precision.HIGHEST


def reduced_factors(count, load, store):
    one = None
    b = None
    forward = []
    for j in range(count):
        left, right, shared = load(j)
        if b is None:
            b = jnp.zeros_like(left)
            one = jnp.ones_like(left)
        store("b", j, b)
        a1 = shared / (one - left * b)
        a2 = a1 * b
        store("a1", j, a1)
        store("a2", j, a2)
        b = right + a2 * shared
        forward.append(b)
    store("b", count, b)
    d = jnp.zeros_like(b)
    store("d", count, d)
    store("g", count, one)
    for j in reversed(range(count)):
        left, right, shared = load(j)
        c1 = shared / (one - right * d)
        c2 = c1 * d
        store("c1", j, c1)
        store("c2", j, c2)
        d = left + c2 * shared
        store("d", j, d)
        before = forward[j - 1] if j else jnp.zeros_like(d)
        store("g", j, one / (one - before * d))


def running(count, first, second, value, phi, psi, scale, keep, emit):
    total = [None]

    def down(i):
        if i == count - 1:
            total[0] = jnp.zeros_like(scale)
        keep(i, total[0])
        total[0] = total[0] + second(i) * value(i)

    def up(i):
        if i == 0:
            total[0] = jnp.zeros_like(scale)
        total[0] = total[0] + first(i) * value(i)
        emit(i, scale * (psi(i) * total[0] + phi(i) * keep(i)))

    downs = [functools.partial(down, i) for i in reversed(range(count))]
    return downs + [functools.partial(up, i) for i in range(count)]


def kernel(
    nx, nz, n_pl, n_xs,
    source_hbm, vertical_hbm, north_hbm, east_hbm, out_ref,
    source, vertical, north, east,
    z_phi, z_psi, z_first, z_second, z_rate, z_hold,
    y_rate, y_phi, y_psi, y_first, y_second, y_value, y_part,
    x_phi, x_psi, x_phi2, x_psi2, x_first, x_second, x_first2, x_second2,
    x_part, x_part2, plane, hold,
    y_coef, y_ends, y_ends2, x_coef, x_two_coef, x_chip_coef, x_ends, x_two, x_chip,
    x_outside, x_back, x_back_in, x_meet, y_fac, y_scan, x_fac,
    load_sem, send_sem, recv_sem,
):
    lines = nx * nz
    blocks = lines // LANES
    pitch, wide = nz + Z_SPARE, LANES // nz
    pl_me, xs_me = lax.axis_index("pl"), lax.axis_index("xs")

    loads = []
    for slot, (hbm, vmem) in enumerate(
        ((north_hbm, north), (vertical_hbm, vertical), (source_hbm, source), (east_hbm, east))
    ):
        vmem = vmem.at[:, pl.ds(0, nz)] if len(vmem.shape) == 3 else vmem
        copy = pltpu.make_async_copy(hbm, vmem, load_sem.at[slot])
        copy.start()
        loads.append(copy)

    side, chips, half = math.isqrt(n_pl), n_xs // 2, nz // 2
    pl_row, pl_col = pl_me // side, lax.rem(pl_me, side)
    chip, core = xs_me // 2, lax.rem(xs_me, 2)
    other = 1 - core

    def ring(offset, count):
        return min(offset, count - offset)

    steps = [(r, c) for r in range(side) for c in range(side) if r or c]
    steps.sort(key=lambda step: -ring(step[0], side) - ring(step[1], side))
    pl_peers = [lax.rem(pl_row + r, side) * side + lax.rem(pl_col + c, side) for r, c in steps]
    ring_offsets = sorted(range(1, chips), key=lambda offset: -ring(offset, chips))
    ring_peers = [lax.rem(chip + offset, chips) * 2 + core for offset in ring_offsets]
    mate = [chip * 2 + other]

    barrier = pltpu.get_barrier_semaphore()
    for axis, peers in (("pl", pl_peers), ("xs", ring_peers + mate)):
        for peer in peers:
            pl.semaphore_signal(barrier, 1, device_id={axis: peer}, device_id_type=MESH)

    def share(axis, slot, peers, source_ref, landing_ref):
        for peer in peers:
            pltpu.make_async_remote_copy(
                src_ref=source_ref,
                dst_ref=landing_ref,
                send_sem=send_sem.at[slot],
                recv_sem=recv_sem.at[slot],
                device_id={axis: peer},
                device_id_type=MESH,
            ).start()

    def arrived(slot, landing, sem=None):
        sem = recv_sem if sem is None else sem
        pltpu.make_async_copy(landing, landing, sem.at[slot]).wait()

    def others(landing):
        return landing.at[pl.ds(0, landing.shape[0] - 1)]

    def rows(b):
        return pl.ds(b * Y_PITCH, LANES)

    def across(y):
        return pl.ds(y, blocks, stride=Y_PITCH)

    def level(z):
        return pl.ds(z, nx, stride=pitch)

    def plane_step(i):
        return pl.ds(i * pitch, nz)

    z_state = [jnp.ones((nx, LANES), jnp.float32)] * 4
    z_steps = []

    def z_invert(z):
        z_rate[z] = 1.0 / vertical[:, z]

    def z_sweep(z):
        phi, phi_step, psi, psi_step = z_state
        back = nz - 1 - z
        z_phi[z] = phi
        z_psi[back] = psi
        phi_flux, psi_flux = phi * z_rate[z], psi * z_rate[back]
        z_first[z] = phi_flux
        z_second[back] = psi_flux
        phi_step = phi_step + phi_flux
        psi_step = psi_step + psi_flux
        z_state[:] = [phi + phi_step, phi_step, psi + psi_step, psi_step]

    def z_solve(z_inv, read, write):
        def keep(z, value=None):
            if value is None:
                return x_part2[pl.ds(z * nx, nx)]
            x_part2[pl.ds(z * nx, nx)] = value

        return running(
            nz, lambda z: z_first[z], lambda z: z_second[z], read, lambda z: z_phi[z], lambda z: z_psi[z],
            z_inv, keep, write,
        )

    def z_first_solve():
        z_hold[...] = 1.0 / z_state[0]

        def to_plane(z, value):
            plane[level(z)] = value

        z_steps.extend(z_solve(z_hold[...], lambda z: source[:, z], to_plane))
        z_steps.extend(functools.partial(y_turn, b) for b in range(blocks))

    def y_turn(b):
        y_value[rows(b)] = jnp.concatenate(
            [plane[plane_step(b * wide + i)] for i in range(wide)], axis=0
        ).T

    for z in range(nz // 2):
        for at in (z, nz - 1 - z):
            z_steps.append(functools.partial(z_invert, at))
    z_steps.extend(functools.partial(z_sweep, z) for z in range(nz))
    z_steps.append(z_first_solve)

    for copy in loads[:3]:
        copy.wait()
    for b in range(blocks):
        y_rate[rows(b)] = (1.0 / north[b * LANES:(b + 1) * LANES]).T

    unit = jnp.ones((blocks, LANES), jnp.float32)
    phi, phi_step, psi, psi_step = unit, unit, unit, unit
    for i in range(LANES):
        back = LANES - 1 - i
        y_phi[across(i)] = phi
        y_psi[across(back)] = psi
        phi_flux, psi_flux = phi * y_rate[across(i)], psi * y_rate[across(back)]
        y_first[across(i)] = phi_flux
        y_second[across(back)] = psi_flux
        phi_step = phi_step + phi_flux
        psi_step = psi_step + psi_flux
        phi = phi + phi_step
        psi = psi + psi_step
        if z_steps and i % 16 < 10:
            z_steps.pop(0)()
    while z_steps:
        z_steps.pop(0)()
    y_inv = 1.0 / phi
    hold[pl.ds(2 * blocks, blocks)] = y_inv
    y_coef[pl_me, 0] = y_psi[across(0)] * y_inv
    y_coef[pl_me, 1] = y_phi[across(LANES - 1)] * y_inv
    y_coef[pl_me, 2] = y_inv

    low = lax.broadcasted_iota(jnp.int32, (LANES, LANES), 0)
    high = lax.broadcasted_iota(jnp.int32, (LANES, LANES), 1)
    upto = jnp.where(high <= low, 1.0, 0.0)
    beyond = jnp.where(high > low, 1.0, 0.0)

    def y_inv_row(b):
        return hold[2 * blocks + b:2 * blocks + b + 1]

    def y_ends_of(ends):
        for b in range(blocks):
            value = y_value[rows(b)]
            second = y_second[rows(b)] * value
            first = y_first[rows(b)] * value
            y_value[rows(b)] = first
            y_part[rows(b)] = second
            ends[pl_me, 0, b:b + 1] = jnp.sum(second, axis=0, keepdims=True) * y_inv_row(b)
            ends[pl_me, 1, b:b + 1] = jnp.sum(first, axis=0, keepdims=True) * y_inv_row(b)

    def y_local():
        for b in range(blocks):
            below = jnp.dot(upto, y_value[rows(b)], precision=HIGHEST, preferred_element_type=jnp.float32)
            above = jnp.dot(beyond, y_part[rows(b)], precision=HIGHEST, preferred_element_type=jnp.float32)
            y_part[rows(b)] = (y_psi[rows(b)] * below + y_phi[rows(b)] * above) * y_inv_row(b)

    def y_finish(slot, ends):
        arrived(slot, others(ends))
        a = c = jnp.zeros((blocks, LANES), jnp.float32)
        y_scan[0, 0] = a
        y_scan[1, n_pl] = c
        for j in range(n_pl):
            k = n_pl - 1 - j
            a = ends[j, 1] + y_fac[2, j] * ends[j, 0] + y_fac[1, j] * a
            c = ends[k, 0] + y_fac[4, k] * ends[k, 1] + y_fac[3, k] * c
            y_scan[0, j + 1] = a
            y_scan[1, k] = c
        a_here, a_next = y_scan[0, pl_me], y_scan[0, pl_me + 1]
        c_here, c_next = y_scan[1, pl_me], y_scan[1, pl_me + 1]
        outside_low = (a_here + y_fac[0, pl_me] * c_here) * y_fac[6, pl_me]
        outside_high = (c_next + y_fac[5, pl_me + 1] * a_next) * y_fac[6, pl_me + 1]
        inv = y_coef[pl_me, 2]
        hold[pl.ds(0, blocks)] = outside_low * inv
        hold[pl.ds(blocks, blocks)] = outside_high * inv
        for b in range(blocks):
            solved = (
                y_part[rows(b)]
                + y_psi[rows(b)] * hold[b:b + 1]
                + y_phi[rows(b)] * hold[blocks + b:blocks + b + 1]
            )
            solved = solved.T
            for i in range(wide):
                plane[plane_step(b * wide + i)] = solved[i * nz:(i + 1) * nz]

    y_ends_of(y_ends)

    def step(i):
        return pl.ds(i * nz, nz)

    loads[3].wait()
    phi = jnp.ones((nz, LANES), jnp.float32)
    phi_step = psi = psi_step = phi
    for i in range(nx // 2):
        for at in (i, nx - 1 - i):
            east[step(at)] = 1.0 / east[step(at)]
    for i in range(nx):
        back = nx - 1 - i
        x_phi[step(i)] = phi
        x_psi[step(back)] = psi
        phi_flux, psi_flux = phi * east[step(i)], psi * east[step(back)]
        x_first[step(i)] = phi_flux
        x_second[step(back)] = psi_flux
        phi_step = phi_step + phi_flux
        psi_step = psi_step + psi_flux
        phi = phi + phi_step
        psi = psi + psi_step
    x_inv = 1.0 / phi

    def x_solve(read, write, spare=None):
        spare = x_part2 if spare is None else spare

        def keep(i, value=None):
            if value is None:
                return spare[step(i)]
            spare[step(i)] = value

        return running(
            nx, lambda i: x_first[step(i)], lambda i: x_second[step(i)], read,
            lambda i: x_phi[step(i)], lambda i: x_psi[step(i)], x_inv, keep, write,
        )

    def into(ref):
        def write(i, value):
            ref[step(i)] = value

        return write

    for one, two in zip(
        x_solve(lambda i: x_phi[step(i)], into(x_phi2)),
        x_solve(lambda i: x_psi[step(i)], into(x_psi2), x_part),
    ):
        one()
        two()
    for i in range(nx):
        x_first2[step(i)] = x_phi2[step(i)] * east[step(i)]
        x_second2[step(i)] = x_psi2[step(i)] * east[step(i)]
    last = step(nx - 1)
    coefficients = (
        x_psi[step(0)] * x_inv, x_phi[last] * x_inv, x_inv,
        x_psi2[step(0)] * x_inv, x_phi2[last] * x_inv, x_phi2[step(0)] * x_inv,
    )
    for q, value in enumerate(coefficients):
        x_coef[0, q] = value[:half]
        x_coef[1, q] = value[half:]
    x_two_coef[core] = x_coef[core]
    pl.semaphore_wait(barrier, n_pl + chips - 1)
    share("xs", 2, mate, x_coef.at[other], x_two_coef.at[core])
    share("pl", 0, pl_peers, y_coef.at[pl_me], y_coef.at[pl_me])
    share("pl", 1, pl_peers, y_ends.at[pl_me], y_ends.at[pl_me])

    y_local()

    arrived(2, x_two_coef.at[0])
    left_a, right_a, shared_a, left2_a, right2_a, shared2_a = (x_two_coef[0, q] for q in range(6))
    left_b, right_b, shared_b, left2_b, right2_b, shared2_b = (x_two_coef[1, q] for q in range(6))
    meet = 1.0 / (1.0 - right_a * left_b)
    last_low, last_high = meet * shared_a, meet * right_a * shared_b
    first_low, first_high = meet * left_b * shared_a, meet * shared_b
    x_meet[0] = meet
    for q, value in enumerate((last_low, last_high, first_low, first_high)):
        x_meet[q + 1] = value

    def joined(p0a, pna, p0b, pnb):
        return (
            p0a + shared_a * (meet * (p0b + left_b * pna)),
            pnb + shared_b * (meet * (pna + right_a * p0b)),
        )

    first_from_low, _ = joined(
        left2_a + shared2_a * first_low, shared2_a + right2_a * first_low,
        left2_b * last_low, shared2_b * last_low,
    )
    first_from_high, last_from_high = joined(
        shared2_a * first_high, right2_a * first_high,
        left2_b * last_high + shared2_b, shared2_b * last_high + right2_b,
    )
    merged = (
        left_a + shared_a * first_low, right_b + shared_b * last_high, shared_a * first_high,
        first_from_low, last_from_high, first_from_high,
    )
    for q, value in enumerate(merged):
        x_chip_coef[chip, q] = value
    share("xs", 3, ring_peers, x_chip_coef.at[chip], x_chip_coef.at[chip])

    names = {"b": 0, "a1": 1, "a2": 2, "c1": 3, "c2": 4, "d": 5, "g": 6}
    arrived(0, others(y_coef))

    def y_store(name, j, value):
        y_fac[names[name], j] = value

    reduced_factors(n_pl, lambda j: (y_coef[j, 0], y_coef[j, 1], y_coef[j, 2]), y_store)
    y_finish(1, y_ends)

    p0 = pn = q0 = qn = jnp.zeros((nz, LANES), jnp.float32)
    for i in range(nx):
        value = plane[plane_step(i)]
        p0 = p0 + x_second[step(i)] * value
        pn = pn + x_first[step(i)] * value
        q0 = q0 + x_second2[step(i)] * value
        qn = qn + x_first2[step(i)] * value
    for q, value in enumerate((p0, pn, q0, qn)):
        x_ends[0, q] = value[:half] * x_inv[:half]
        x_ends[1, q] = value[half:] * x_inv[half:]
    share("xs", 4, mate, x_ends.at[other], x_two.at[core])
    x_two[core] = x_ends[core]

    for run in x_solve(lambda i: plane[plane_step(i)], into(x_part)):
        run()

    arrived(4, x_two.at[0])
    left_a, right_a, shared_a, left2_a, right2_a, shared2_a = (x_two_coef[0, q] for q in range(6))
    left_b, right_b, shared_b, left2_b, right2_b, shared2_b = (x_two_coef[1, q] for q in range(6))
    meet, last_low, last_high, first_low, first_high = (x_meet[q] for q in range(5))

    def border(p0b, pna):
        return meet * (pna + right_a * p0b), meet * (p0b + left_b * pna)

    def ends_again(last_a, first_b, low, high):
        p0a, pna = x_two[0, 2] + shared2_a * first_b, x_two[0, 3] + right2_a * first_b
        p0b, pnb = x_two[1, 2] + left2_b * last_a, x_two[1, 3] + shared2_b * last_a
        if low is not None:
            p0a, pna = p0a + left2_a * low, pna + shared2_a * low
            p0b, pnb = p0b + shared2_b * high, pnb + right2_b * high
        return p0a, pna, p0b, pnb

    last_a, first_b = border(x_two[1, 0], x_two[0, 1])
    x_chip[chip, 0] = x_two[0, 0] + shared_a * first_b
    x_chip[chip, 1] = x_two[1, 1] + shared_b * last_a
    p0a, pna, p0b, pnb = ends_again(last_a, first_b, None, None)
    last2, first2 = border(p0b, pna)
    x_chip[chip, 2] = p0a + shared_a * first2
    x_chip[chip, 3] = pnb + shared_b * last2
    share("xs", 5, ring_peers, x_chip.at[chip], x_chip.at[chip])

    arrived(3, others(x_chip_coef))

    def x_store(name, j, value):
        x_fac[names[name], j] = value

    reduced_factors(
        chips, lambda j: (x_chip_coef[j, 0], x_chip_coef[j, 1], x_chip_coef[j, 2]), x_store
    )
    for run in x_solve(lambda i: x_part[step(i)], into(x_part)):
        run()

    arrived(5, others(x_chip))

    def fac(name, j):
        return x_fac[names[name], j]

    def x_reduced(ends):
        a = c = jnp.zeros((half, LANES), jnp.float32)
        lefts, rights = [a], [c]
        for j in range(chips):
            k = chips - 1 - j
            a = ends[j][1] + fac("a2", j) * ends[j][0] + fac("a1", j) * a
            c = ends[k][0] + fac("c2", k) * ends[k][1] + fac("c1", k) * c
            lefts.append(a)
            rights.append(c)
        rights = rights[::-1]
        lows = [(lefts[j] + fac("b", j) * rights[j]) * fac("g", j) for j in range(chips)]
        highs = [
            (rights[j + 1] + fac("d", j + 1) * lefts[j + 1]) * fac("g", j + 1) for j in range(chips)
        ]
        return lows, highs

    lows, highs = x_reduced([(x_chip[j, 0], x_chip[j, 1]) for j in range(chips)])
    again = []
    for j in range(chips):
        left, right, shared = (x_chip_coef[j, q] for q in range(3, 6))
        again.append(
            (
                x_chip[j, 2] + left * lows[j] + shared * highs[j],
                x_chip[j, 3] + shared * lows[j] + right * highs[j],
            )
        )
    lows2, highs2 = x_reduced(again)
    for j in range(chips):
        for q, value in enumerate((lows[j], highs[j], lows2[j], highs2[j])):
            x_outside[j, q] = value
    low, high, low2, high2 = (x_outside[chip, q] for q in range(4))
    last_a, first_b = border(x_two[1, 0], x_two[0, 1])
    last_a = last_a + last_low * low + last_high * high
    first_b = first_b + first_low * low + first_high * high
    p0a, pna, p0b, pnb = ends_again(last_a, first_b, low, high)
    last2, first2 = border(p0b, pna)
    last2 = last2 + last_low * low2 + last_high * high2
    first2 = first2 + first_low * low2 + first_high * high2
    for q, value in enumerate((low, first_b, low2, first2)):
        x_back[0, q] = value
    for q, value in enumerate((last_a, high, last2, high2)):
        x_back[1, q] = value
    share("xs", 6, mate, x_back.at[other], x_back_in.at[core])
    x_back_in[core] = x_back[core]

    arrived(6, x_back_in.at[0])
    low1, high1, low2, high2 = (
        jnp.concatenate([x_back_in[0, q], x_back_in[1, q]], axis=0) * x_inv for q in range(4)
    )
    for i in range(nx):
        plane[plane_step(i)] = (
            x_part[step(i)]
            + x_psi2[step(i)] * low1
            + x_phi2[step(i)] * high1
            + x_psi[step(i)] * low2
            + x_phi[step(i)] * high2
        )

    for b in range(blocks):
        y_turn(b)
    y_ends_of(y_ends2)
    share("pl", 7, pl_peers, y_ends2.at[pl_me], y_ends2.at[pl_me])
    y_local()
    y_finish(7, y_ends2)

    def to_out(z, value):
        out_ref[pl.ds(z, nx, stride=nz)] = value

    for run in z_solve(z_hold[...], lambda z: plane[level(z)], to_out):
        run()

    for slot, landing in enumerate(
        (
            others(y_coef), others(y_ends), x_two_coef.at[0], others(x_chip_coef),
            x_two.at[0], others(x_chip), x_back_in.at[0], others(y_ends2),
        )
    ):
        arrived(slot, landing, send_sem)


def shards(n_pl, n_xs, source, eastward_rate, northward_rate, vertical_rate, amplitude):
    nx, nz, ny = source.shape
    lines = nx * nz
    blocks = lines // LANES
    chips, half = n_xs // 2, nz // 2
    here = lambda array: pltpu.with_memory_space_constraint(array, pltpu.HBM)
    flat = lambda array: here(array.reshape(lines, ny))
    field = pltpu.VMEM((lines, LANES), jnp.float32)
    padded = pltpu.VMEM((nx, nz + Z_SPARE, LANES), jnp.float32)
    turned = pltpu.VMEM((blocks * Y_PITCH, LANES), jnp.float32)
    column = pltpu.VMEM((nz, nx, LANES), jnp.float32)
    vmem = lambda *shape: pltpu.VMEM(shape, jnp.float32)
    second = pl.pallas_call(
        functools.partial(kernel, nx, nz, n_pl, n_xs),
        out_shape=jax.ShapeDtypeStruct((lines, ny), jnp.float32),
        in_specs=[pl.BlockSpec(memory_space=pltpu.HBM)] * 4,
        out_specs=pl.BlockSpec(memory_space=pltpu.VMEM),
        scratch_shapes=[padded, padded, field, field]
        + [column] * 5
        + [vmem(nx, LANES)]
        + [turned] * 7
        + [field] * 8
        + [field] * 2
        + [vmem(nx * (nz + Z_SPARE), LANES)]
        + [vmem(3 * blocks, LANES)]
        + [
            vmem(n_pl, 3, blocks, LANES),
            vmem(n_pl, 2, blocks, LANES),
            vmem(n_pl, 2, blocks, LANES),
            vmem(2, 6, half, LANES),
            vmem(2, 6, half, LANES),
            vmem(chips, 6, half, LANES),
            vmem(2, 4, half, LANES),
            vmem(2, 4, half, LANES),
            vmem(chips, 4, half, LANES),
            vmem(chips, 4, half, LANES),
            vmem(2, 4, half, LANES),
            vmem(2, 4, half, LANES),
            vmem(5, half, LANES),
            vmem(7, n_pl + 1, blocks, LANES),
            vmem(2, n_pl + 1, blocks, LANES),
            vmem(7, chips + 1, half, LANES),
            pltpu.SemaphoreType.DMA((4,)),
            pltpu.SemaphoreType.DMA((8,)),
            pltpu.SemaphoreType.DMA((8,)),
        ],
        compiler_params=pltpu.CompilerParams(
            collective_id=0, has_side_effects=True, vmem_limit_bytes=40 * 1024 * 1024
        ),
        name="adi",
    )(here(source), here(vertical_rate), flat(northward_rate), flat(eastward_rate))
    return amplitude * second.reshape(nx, nz, ny)


def solution(mesh):
    spec = P("xs", None, "pl")
    return jax.shard_map(
        functools.partial(shards, mesh.shape["pl"], mesh.shape["xs"]),
        mesh=mesh,
        in_specs=(spec,) * 5,
        out_specs=spec,
        check_vma=False,
    )
```

```python
import functools
import math

import jax
import jax.numpy as jnp
from jax import lax
from jax.experimental import pallas as pl
from jax.experimental.pallas import tpu as pltpu
from jax.sharding import PartitionSpec as P

MESH = pl.DeviceIdType.MESH
LANES = 128
Y_PITCH = LANES + 8
Z_SPARE = 8
HIGHEST = lax.Precision.HIGHEST


def reduced_factors(count, load, store):
    one = None
    b = None
    forward = []
    for j in range(count):
        left, right, shared = load(j)
        if b is None:
            b = jnp.zeros_like(left)
            one = jnp.ones_like(left)
        store("b", j, b)
        a1 = shared / (one - left * b)
        a2 = a1 * b
        store("a1", j, a1)
        store("a2", j, a2)
        b = right + a2 * shared
        forward.append(b)
    store("b", count, b)
    d = jnp.zeros_like(b)
    store("d", count, d)
    store("g", count, one)
    for j in reversed(range(count)):
        left, right, shared = load(j)
        c1 = shared / (one - right * d)
        c2 = c1 * d
        store("c1", j, c1)
        store("c2", j, c2)
        d = left + c2 * shared
        store("d", j, d)
        before = forward[j - 1] if j else jnp.zeros_like(d)
        store("g", j, one / (one - before * d))


def running(count, first, second, value, phi, psi, scale, keep, emit):
    total = [None]

    def down(i):
        if i == count - 1:
            total[0] = jnp.zeros_like(scale)
        keep(i, total[0])
        total[0] = total[0] + second(i) * value(i)

    def up(i):
        if i == 0:
            total[0] = jnp.zeros_like(scale)
        total[0] = total[0] + first(i) * value(i)
        emit(i, scale * (psi(i) * total[0] + phi(i) * keep(i)))

    downs = [functools.partial(down, i) for i in reversed(range(count))]
    return downs + [functools.partial(up, i) for i in range(count)]


def kernel(
    nx, nz, n_pl, n_xs,
    source_hbm, vertical_hbm, north_hbm, east_hbm, out_ref,
    source, vertical, north, east,
    z_phi, z_psi, z_first, z_second, z_rate, z_hold,
    y_rate, y_phi, y_psi, y_first, y_second, y_value, y_part,
    x_phi, x_psi, x_phi2, x_psi2, x_first, x_second, x_first2, x_second2,
    x_part, x_part2, plane, hold,
    y_coef, y_ends, y_ends2, x_coef, x_two_coef, x_chip_coef, x_ends, x_two, x_chip,
    x_outside, x_back, x_back_in, x_meet, y_fac, y_scan, x_fac,
    load_sem, send_sem, recv_sem,
):
    lines = nx * nz
    blocks = lines // LANES
    pitch, wide = nz + Z_SPARE, LANES // nz
    pl_me, xs_me = lax.axis_index("pl"), lax.axis_index("xs")

    loads = []
    for slot, (hbm, vmem) in enumerate(
        ((north_hbm, north), (vertical_hbm, vertical), (source_hbm, source), (east_hbm, east))
    ):
        vmem = vmem.at[:, pl.ds(0, nz)] if len(vmem.shape) == 3 else vmem
        copy = pltpu.make_async_copy(hbm, vmem, load_sem.at[slot])
        copy.start()
        loads.append(copy)

    side, chips, half = math.isqrt(n_pl), n_xs // 2, nz // 2
    pl_row, pl_col = pl_me // side, lax.rem(pl_me, side)
    chip, core = xs_me // 2, lax.rem(xs_me, 2)
    other = 1 - core

    def ring(offset, count):
        return min(offset, count - offset)

    steps = [(r, c) for r in range(side) for c in range(side) if r or c]
    steps.sort(key=lambda step: -ring(step[0], side) - ring(step[1], side))
    pl_peers = [lax.rem(pl_row + r, side) * side + lax.rem(pl_col + c, side) for r, c in steps]
    ring_offsets = sorted(range(1, chips), key=lambda offset: -ring(offset, chips))
    ring_peers = [lax.rem(chip + offset, chips) * 2 + core for offset in ring_offsets]
    mate = [chip * 2 + other]

    barrier = pltpu.get_barrier_semaphore()
    for axis, peers in (("pl", pl_peers), ("xs", ring_peers + mate)):
        for peer in peers:
            pl.semaphore_signal(barrier, 1, device_id={axis: peer}, device_id_type=MESH)

    def share(axis, slot, peers, source_ref, landing_ref):
        for peer in peers:
            pltpu.make_async_remote_copy(
                src_ref=source_ref,
                dst_ref=landing_ref,
                send_sem=send_sem.at[slot],
                recv_sem=recv_sem.at[slot],
                device_id={axis: peer},
                device_id_type=MESH,
            ).start()

    def arrived(slot, landing, sem=None):
        sem = recv_sem if sem is None else sem
        pltpu.make_async_copy(landing, landing, sem.at[slot]).wait()

    def others(landing):
        return landing.at[pl.ds(0, landing.shape[0] - 1)]

    def rows(b):
        return pl.ds(b * Y_PITCH, LANES)

    def across(y):
        return pl.ds(y, blocks, stride=Y_PITCH)

    def level(z):
        return pl.ds(z, nx, stride=pitch)

    def plane_step(i):
        return pl.ds(i * pitch, nz)

    z_state = [jnp.ones((nx, LANES), jnp.float32)] * 4
    z_steps = []

    def z_invert(z):
        z_rate[z] = 1.0 / vertical[:, z]

    def z_sweep(z):
        phi, phi_step, psi, psi_step = z_state
        back = nz - 1 - z
        z_phi[z] = phi
        z_psi[back] = psi
        phi_flux, psi_flux = phi * z_rate[z], psi * z_rate[back]
        z_first[z] = phi_flux
        z_second[back] = psi_flux
        phi_step = phi_step + phi_flux
        psi_step = psi_step + psi_flux
        z_state[:] = [phi + phi_step, phi_step, psi + psi_step, psi_step]

    def z_solve(z_inv, read, write, start=0, count=nx):
        group = pl.ds(start, count)

        def keep(z, value=None):
            if value is None:
                return x_part2[pl.ds(z * nx + start, count)]
            x_part2[pl.ds(z * nx + start, count)] = value

        return running(
            nz, lambda z: z_first[z, group], lambda z: z_second[z, group], read,
            lambda z: z_phi[z, group], lambda z: z_psi[z, group], z_inv, keep, write,
        )

    def z_first_solve():
        z_hold[...] = 1.0 / z_state[0]

        def to_plane(z, value):
            plane[level(z)] = value

        z_steps.extend(z_solve(z_hold[...], lambda z: source[:, z], to_plane))
        z_steps.extend(functools.partial(y_turn, b) for b in range(blocks))

    def y_turn(b):
        y_value[rows(b)] = jnp.concatenate(
            [plane[plane_step(b * wide + i)] for i in range(wide)], axis=0
        ).T

    for z in range(nz // 2):
        for at in (z, nz - 1 - z):
            z_steps.append(functools.partial(z_invert, at))
    z_steps.extend(functools.partial(z_sweep, z) for z in range(nz))
    z_steps.append(z_first_solve)

    for copy in loads[:3]:
        copy.wait()
    for b in range(blocks):
        y_rate[rows(b)] = (1.0 / north[b * LANES:(b + 1) * LANES]).T

    unit = jnp.ones((blocks, LANES), jnp.float32)
    phi, phi_step, psi, psi_step = unit, unit, unit, unit
    for i in range(LANES):
        back = LANES - 1 - i
        y_phi[across(i)] = phi
        y_psi[across(back)] = psi
        phi_flux, psi_flux = phi * y_rate[across(i)], psi * y_rate[across(back)]
        y_first[across(i)] = phi_flux
        y_second[across(back)] = psi_flux
        phi_step = phi_step + phi_flux
        psi_step = psi_step + psi_flux
        phi = phi + phi_step
        psi = psi + psi_step
        if z_steps and i % 16 < 10:
            z_steps.pop(0)()
    while z_steps:
        z_steps.pop(0)()
    y_inv = 1.0 / phi
    hold[pl.ds(2 * blocks, blocks)] = y_inv
    y_coef[pl_me, 0] = y_psi[across(0)] * y_inv
    y_coef[pl_me, 1] = y_phi[across(LANES - 1)] * y_inv
    y_coef[pl_me, 2] = y_inv

    low = lax.broadcasted_iota(jnp.int32, (LANES, LANES), 0)
    high = lax.broadcasted_iota(jnp.int32, (LANES, LANES), 1)
    upto = jnp.where(high <= low, 1.0, 0.0)
    beyond = jnp.where(high > low, 1.0, 0.0)

    def y_inv_row(b):
        return hold[2 * blocks + b:2 * blocks + b + 1]

    def y_ends_of(ends):
        for b in range(blocks):
            value = y_value[rows(b)]
            second = y_second[rows(b)] * value
            first = y_first[rows(b)] * value
            y_value[rows(b)] = first
            y_part[rows(b)] = second
            ends[pl_me, 0, b:b + 1] = jnp.sum(second, axis=0, keepdims=True) * y_inv_row(b)
            ends[pl_me, 1, b:b + 1] = jnp.sum(first, axis=0, keepdims=True) * y_inv_row(b)

    def y_local():
        for b in range(blocks):
            below = jnp.dot(upto, y_value[rows(b)], precision=HIGHEST, preferred_element_type=jnp.float32)
            above = jnp.dot(beyond, y_part[rows(b)], precision=HIGHEST, preferred_element_type=jnp.float32)
            y_part[rows(b)] = (y_psi[rows(b)] * below + y_phi[rows(b)] * above) * y_inv_row(b)

    def y_finish(slot, ends, consume):
        arrived(slot, others(ends))
        a = c = jnp.zeros((blocks, LANES), jnp.float32)
        y_scan[0, 0] = a
        y_scan[1, n_pl] = c
        for j in range(n_pl):
            k = n_pl - 1 - j
            a = ends[j, 1] + y_fac[2, j] * ends[j, 0] + y_fac[1, j] * a
            c = ends[k, 0] + y_fac[4, k] * ends[k, 1] + y_fac[3, k] * c
            y_scan[0, j + 1] = a
            y_scan[1, k] = c
        a_here, a_next = y_scan[0, pl_me], y_scan[0, pl_me + 1]
        c_here, c_next = y_scan[1, pl_me], y_scan[1, pl_me + 1]
        outside_low = (a_here + y_fac[0, pl_me] * c_here) * y_fac[6, pl_me]
        outside_high = (c_next + y_fac[5, pl_me + 1] * a_next) * y_fac[6, pl_me + 1]
        inv = y_coef[pl_me, 2]
        hold[pl.ds(0, blocks)] = outside_low * inv
        hold[pl.ds(blocks, blocks)] = outside_high * inv
        for b in range(blocks):
            solved = (
                y_part[rows(b)]
                + y_psi[rows(b)] * hold[b:b + 1]
                + y_phi[rows(b)] * hold[blocks + b:blocks + b + 1]
            )
            solved = solved.T
            for i in range(wide):
                plane[plane_step(b * wide + i)] = solved[i * nz:(i + 1) * nz]
            consume(b, solved)

    y_ends_of(y_ends)

    def step(i):
        return pl.ds(i * nz, nz)

    loads[3].wait()
    phi = jnp.ones((nz, LANES), jnp.float32)
    phi_step = psi = psi_step = phi
    for i in range(nx // 2):
        for at in (i, nx - 1 - i):
            east[step(at)] = 1.0 / east[step(at)]
    for i in range(nx):
        back = nx - 1 - i
        x_phi[step(i)] = phi
        x_psi[step(back)] = psi
        phi_flux, psi_flux = phi * east[step(i)], psi * east[step(back)]
        x_first[step(i)] = phi_flux
        x_second[step(back)] = psi_flux
        phi_step = phi_step + phi_flux
        psi_step = psi_step + psi_flux
        phi = phi + phi_step
        psi = psi + psi_step
    x_inv = 1.0 / phi

    def x_solve(read, write, spare=None):
        spare = x_part2 if spare is None else spare

        def keep(i, value=None):
            if value is None:
                return spare[step(i)]
            spare[step(i)] = value

        return running(
            nx, lambda i: x_first[step(i)], lambda i: x_second[step(i)], read,
            lambda i: x_phi[step(i)], lambda i: x_psi[step(i)], x_inv, keep, write,
        )

    def into(ref):
        def write(i, value):
            ref[step(i)] = value

        return write

    for one, two in zip(
        x_solve(lambda i: x_phi[step(i)], into(x_phi2)),
        x_solve(lambda i: x_psi[step(i)], into(x_psi2), x_part),
    ):
        one()
        two()
    for i in range(nx):
        x_first2[step(i)] = x_phi2[step(i)] * east[step(i)]
        x_second2[step(i)] = x_psi2[step(i)] * east[step(i)]
    last = step(nx - 1)
    coefficients = (
        x_psi[step(0)] * x_inv, x_phi[last] * x_inv, x_inv,
        x_psi2[step(0)] * x_inv, x_phi2[last] * x_inv, x_phi2[step(0)] * x_inv,
    )
    for q, value in enumerate(coefficients):
        x_coef[0, q] = value[:half]
        x_coef[1, q] = value[half:]
    x_two_coef[core] = x_coef[core]
    pl.semaphore_wait(barrier, n_pl + chips - 1)
    share("xs", 2, mate, x_coef.at[other], x_two_coef.at[core])
    share("pl", 0, pl_peers, y_coef.at[pl_me], y_coef.at[pl_me])
    share("pl", 1, pl_peers, y_ends.at[pl_me], y_ends.at[pl_me])

    y_local()

    arrived(2, x_two_coef.at[0])
    left_a, right_a, shared_a, left2_a, right2_a, shared2_a = (x_two_coef[0, q] for q in range(6))
    left_b, right_b, shared_b, left2_b, right2_b, shared2_b = (x_two_coef[1, q] for q in range(6))
    meet = 1.0 / (1.0 - right_a * left_b)
    last_low, last_high = meet * shared_a, meet * right_a * shared_b
    first_low, first_high = meet * left_b * shared_a, meet * shared_b
    x_meet[0] = meet
    for q, value in enumerate((last_low, last_high, first_low, first_high)):
        x_meet[q + 1] = value

    def joined(p0a, pna, p0b, pnb):
        return (
            p0a + shared_a * (meet * (p0b + left_b * pna)),
            pnb + shared_b * (meet * (pna + right_a * p0b)),
        )

    first_from_low, _ = joined(
        left2_a + shared2_a * first_low, shared2_a + right2_a * first_low,
        left2_b * last_low, shared2_b * last_low,
    )
    first_from_high, last_from_high = joined(
        shared2_a * first_high, right2_a * first_high,
        left2_b * last_high + shared2_b, shared2_b * last_high + right2_b,
    )
    merged = (
        left_a + shared_a * first_low, right_b + shared_b * last_high, shared_a * first_high,
        first_from_low, last_from_high, first_from_high,
    )
    for q, value in enumerate(merged):
        x_chip_coef[chip, q] = value
    share("xs", 3, ring_peers, x_chip_coef.at[chip], x_chip_coef.at[chip])

    names = {"b": 0, "a1": 1, "a2": 2, "c1": 3, "c2": 4, "d": 5, "g": 6}
    arrived(0, others(y_coef))

    def y_store(name, j, value):
        y_fac[names[name], j] = value

    reduced_factors(n_pl, lambda j: (y_coef[j, 0], y_coef[j, 1], y_coef[j, 2]), y_store)
    sums = [jnp.zeros((nz, LANES), jnp.float32)] * 4

    def add_ends(b, solved):
        for i in range(wide):
            at, value = step(b * wide + i), solved[i * nz:(i + 1) * nz]
            for q, weight in enumerate((x_second, x_first, x_second2, x_first2)):
                sums[q] = sums[q] + weight[at] * value

    y_finish(1, y_ends, add_ends)

    for q, value in enumerate(sums):
        x_ends[0, q] = value[:half] * x_inv[:half]
        x_ends[1, q] = value[half:] * x_inv[half:]
    share("xs", 4, mate, x_ends.at[other], x_two.at[core])
    x_two[core] = x_ends[core]

    for run in x_solve(lambda i: plane[plane_step(i)], into(x_part)):
        run()

    arrived(4, x_two.at[0])
    left_a, right_a, shared_a, left2_a, right2_a, shared2_a = (x_two_coef[0, q] for q in range(6))
    left_b, right_b, shared_b, left2_b, right2_b, shared2_b = (x_two_coef[1, q] for q in range(6))
    meet, last_low, last_high, first_low, first_high = (x_meet[q] for q in range(5))

    def border(p0b, pna):
        return meet * (pna + right_a * p0b), meet * (p0b + left_b * pna)

    def ends_again(last_a, first_b, low, high):
        p0a, pna = x_two[0, 2] + shared2_a * first_b, x_two[0, 3] + right2_a * first_b
        p0b, pnb = x_two[1, 2] + left2_b * last_a, x_two[1, 3] + shared2_b * last_a
        if low is not None:
            p0a, pna = p0a + left2_a * low, pna + shared2_a * low
            p0b, pnb = p0b + shared2_b * high, pnb + right2_b * high
        return p0a, pna, p0b, pnb

    last_a, first_b = border(x_two[1, 0], x_two[0, 1])
    x_chip[chip, 0] = x_two[0, 0] + shared_a * first_b
    x_chip[chip, 1] = x_two[1, 1] + shared_b * last_a
    p0a, pna, p0b, pnb = ends_again(last_a, first_b, None, None)
    last2, first2 = border(p0b, pna)
    x_chip[chip, 2] = p0a + shared_a * first2
    x_chip[chip, 3] = pnb + shared_b * last2
    share("xs", 5, ring_peers, x_chip.at[chip], x_chip.at[chip])

    arrived(3, others(x_chip_coef))

    def x_store(name, j, value):
        x_fac[names[name], j] = value

    reduced_factors(
        chips, lambda j: (x_chip_coef[j, 0], x_chip_coef[j, 1], x_chip_coef[j, 2]), x_store
    )
    for run in x_solve(lambda i: x_part[step(i)], into(x_part)):
        run()

    arrived(5, others(x_chip))

    def fac(name, j):
        return x_fac[names[name], j]

    def x_reduced(ends):
        a = c = jnp.zeros((half, LANES), jnp.float32)
        lefts, rights = [a], [c]
        for j in range(chips):
            k = chips - 1 - j
            a = ends[j][1] + fac("a2", j) * ends[j][0] + fac("a1", j) * a
            c = ends[k][0] + fac("c2", k) * ends[k][1] + fac("c1", k) * c
            lefts.append(a)
            rights.append(c)
        rights = rights[::-1]
        lows = [(lefts[j] + fac("b", j) * rights[j]) * fac("g", j) for j in range(chips)]
        highs = [
            (rights[j + 1] + fac("d", j + 1) * lefts[j + 1]) * fac("g", j + 1) for j in range(chips)
        ]
        return lows, highs

    lows, highs = x_reduced([(x_chip[j, 0], x_chip[j, 1]) for j in range(chips)])
    again = []
    for j in range(chips):
        left, right, shared = (x_chip_coef[j, q] for q in range(3, 6))
        again.append(
            (
                x_chip[j, 2] + left * lows[j] + shared * highs[j],
                x_chip[j, 3] + shared * lows[j] + right * highs[j],
            )
        )
    lows2, highs2 = x_reduced(again)
    for j in range(chips):
        for q, value in enumerate((lows[j], highs[j], lows2[j], highs2[j])):
            x_outside[j, q] = value
    low, high, low2, high2 = (x_outside[chip, q] for q in range(4))
    last_a, first_b = border(x_two[1, 0], x_two[0, 1])
    last_a = last_a + last_low * low + last_high * high
    first_b = first_b + first_low * low + first_high * high
    p0a, pna, p0b, pnb = ends_again(last_a, first_b, low, high)
    last2, first2 = border(p0b, pna)
    last2 = last2 + last_low * low2 + last_high * high2
    first2 = first2 + first_low * low2 + first_high * high2
    for q, value in enumerate((low, first_b, low2, first2)):
        x_back[0, q] = value
    for q, value in enumerate((last_a, high, last2, high2)):
        x_back[1, q] = value
    share("xs", 6, mate, x_back.at[other], x_back_in.at[core])
    x_back_in[core] = x_back[core]

    arrived(6, x_back_in.at[0])
    low1, high1, low2, high2 = (
        jnp.concatenate([x_back_in[0, q], x_back_in[1, q]], axis=0) * x_inv for q in range(4)
    )
    for b in range(blocks):
        pieces = [
            x_part[at]
            + x_psi2[at] * low1
            + x_phi2[at] * high1
            + x_psi[at] * low2
            + x_phi[at] * high2
            for at in (step(b * wide + i) for i in range(wide))
        ]
        y_value[rows(b)] = jnp.concatenate(pieces, axis=0).T
    y_ends_of(y_ends2)
    share("pl", 7, pl_peers, y_ends2.at[pl_me], y_ends2.at[pl_me])
    y_local()
    def finish_z(b, solved):
        start = b * wide

        def read(z):
            return plane[pl.ds(start * pitch + z, wide, stride=pitch)]

        def write(z, value):
            out_ref[pl.ds(start * nz + z, wide, stride=nz)] = value

        for run in z_solve(z_hold[start:start + wide], read, write, start, wide):
            run()

    y_finish(7, y_ends2, finish_z)

    for slot, landing in enumerate(
        (
            others(y_coef), others(y_ends), x_two_coef.at[0], others(x_chip_coef),
            x_two.at[0], others(x_chip), x_back_in.at[0], others(y_ends2),
        )
    ):
        arrived(slot, landing, send_sem)


def shards(n_pl, n_xs, source, eastward_rate, northward_rate, vertical_rate, amplitude):
    nx, nz, ny = source.shape
    lines = nx * nz
    blocks = lines // LANES
    chips, half = n_xs // 2, nz // 2
    here = lambda array: pltpu.with_memory_space_constraint(array, pltpu.HBM)
    flat = lambda array: here(array.reshape(lines, ny))
    field = pltpu.VMEM((lines, LANES), jnp.float32)
    padded = pltpu.VMEM((nx, nz + Z_SPARE, LANES), jnp.float32)
    turned = pltpu.VMEM((blocks * Y_PITCH, LANES), jnp.float32)
    column = pltpu.VMEM((nz, nx, LANES), jnp.float32)
    vmem = lambda *shape: pltpu.VMEM(shape, jnp.float32)
    second = pl.pallas_call(
        functools.partial(kernel, nx, nz, n_pl, n_xs),
        out_shape=jax.ShapeDtypeStruct((lines, ny), jnp.float32),
        in_specs=[pl.BlockSpec(memory_space=pltpu.HBM)] * 4,
        out_specs=pl.BlockSpec(memory_space=pltpu.VMEM),
        scratch_shapes=[padded, padded, field, field]
        + [column] * 5
        + [vmem(nx, LANES)]
        + [turned] * 7
        + [field] * 8
        + [field] * 2
        + [vmem(nx * (nz + Z_SPARE), LANES)]
        + [vmem(3 * blocks, LANES)]
        + [
            vmem(n_pl, 3, blocks, LANES),
            vmem(n_pl, 2, blocks, LANES),
            vmem(n_pl, 2, blocks, LANES),
            vmem(2, 6, half, LANES),
            vmem(2, 6, half, LANES),
            vmem(chips, 6, half, LANES),
            vmem(2, 4, half, LANES),
            vmem(2, 4, half, LANES),
            vmem(chips, 4, half, LANES),
            vmem(chips, 4, half, LANES),
            vmem(2, 4, half, LANES),
            vmem(2, 4, half, LANES),
            vmem(5, half, LANES),
            vmem(7, n_pl + 1, blocks, LANES),
            vmem(2, n_pl + 1, blocks, LANES),
            vmem(7, chips + 1, half, LANES),
            pltpu.SemaphoreType.DMA((4,)),
            pltpu.SemaphoreType.DMA((8,)),
            pltpu.SemaphoreType.DMA((8,)),
        ],
        compiler_params=pltpu.CompilerParams(
            collective_id=0, has_side_effects=True, vmem_limit_bytes=40 * 1024 * 1024
        ),
        name="adi",
    )(here(source), here(vertical_rate), flat(northward_rate), flat(eastward_rate))
    return amplitude * second.reshape(nx, nz, ny)


def solution(mesh):
    spec = P("xs", None, "pl")
    return jax.shard_map(
        functools.partial(shards, mesh.shape["pl"], mesh.shape["xs"]),
        mesh=mesh,
        in_specs=(spec,) * 5,
        out_specs=spec,
        check_vma=False,
    )
```

```python
import functools
import math

import jax
import jax.numpy as jnp
from jax import lax
from jax.experimental import pallas as pl
from jax.experimental.pallas import tpu as pltpu
from jax.sharding import PartitionSpec as P

MESH = pl.DeviceIdType.MESH
LANES = 128
Y_PITCH = LANES + 8
Z_SPARE = 8
HIGHEST = lax.Precision.HIGHEST


def reduced_factors(count, load, store):
    one = None
    b = None
    forward = []
    for j in range(count):
        left, right, shared = load(j)
        if b is None:
            b = jnp.zeros_like(left)
            one = jnp.ones_like(left)
        store("b", j, b)
        a1 = shared / (one - left * b)
        a2 = a1 * b
        store("a1", j, a1)
        store("a2", j, a2)
        b = right + a2 * shared
        forward.append(b)
    store("b", count, b)
    d = jnp.zeros_like(b)
    store("d", count, d)
    store("g", count, one)
    for j in reversed(range(count)):
        left, right, shared = load(j)
        c1 = shared / (one - right * d)
        c2 = c1 * d
        store("c1", j, c1)
        store("c2", j, c2)
        d = left + c2 * shared
        store("d", j, d)
        before = forward[j - 1] if j else jnp.zeros_like(d)
        store("g", j, one / (one - before * d))


def running(count, first, second, value, phi, psi, scale, keep, emit):
    total = [None]

    def down(i):
        if i == count - 1:
            total[0] = jnp.zeros_like(scale)
        keep(i, total[0])
        total[0] = total[0] + second(i) * value(i)

    def up(i):
        if i == 0:
            total[0] = jnp.zeros_like(scale)
        total[0] = total[0] + first(i) * value(i)
        emit(i, scale * (psi(i) * total[0] + phi(i) * keep(i)))

    downs = [functools.partial(down, i) for i in reversed(range(count))]
    return downs + [functools.partial(up, i) for i in range(count)]


def kernel(
    nx, nz, n_pl, n_xs,
    source_hbm, vertical_hbm, north_hbm, east_hbm, out_ref,
    source, vertical, north, east,
    z_phi, z_psi, z_first, z_second, z_rate, z_hold,
    y_rate, y_phi, y_psi, y_first, y_second, y_value, y_part,
    x_phi, x_psi, x_phi2, x_psi2, x_first, x_second, x_first2, x_second2,
    x_part, x_part2, plane, hold,
    y_coef, y_ends, y_ends2, x_coef, x_two_coef, x_chip_coef, x_ends, x_two, x_chip,
    x_outside, x_back, x_back_in, x_meet, y_fac, y_scan, x_fac,
    load_sem, send_sem, recv_sem,
):
    lines = nx * nz
    blocks = lines // LANES
    pitch, wide = nz + Z_SPARE, LANES // nz
    pl_me, xs_me = lax.axis_index("pl"), lax.axis_index("xs")

    loads = []
    for slot, (hbm, vmem) in enumerate(
        ((north_hbm, north), (vertical_hbm, vertical), (source_hbm, source), (east_hbm, east))
    ):
        vmem = vmem.at[:, pl.ds(0, nz)] if len(vmem.shape) == 3 else vmem
        copy = pltpu.make_async_copy(hbm, vmem, load_sem.at[slot])
        copy.start()
        loads.append(copy)

    side, chips, half = math.isqrt(n_pl), n_xs // 2, nz // 2
    pl_row, pl_col = pl_me // side, lax.rem(pl_me, side)
    chip, core = xs_me // 2, lax.rem(xs_me, 2)
    other = 1 - core

    def ring(offset, count):
        return min(offset, count - offset)

    steps = [(r, c) for r in range(side) for c in range(side) if r or c]
    steps.sort(key=lambda step: -ring(step[0], side) - ring(step[1], side))
    pl_peers = [lax.rem(pl_row + r, side) * side + lax.rem(pl_col + c, side) for r, c in steps]
    ring_offsets = sorted(range(1, chips), key=lambda offset: -ring(offset, chips))
    ring_peers = [lax.rem(chip + offset, chips) * 2 + core for offset in ring_offsets]
    mate = [chip * 2 + other]

    barrier = pltpu.get_barrier_semaphore()
    for axis, peers in (("pl", pl_peers), ("xs", ring_peers + mate)):
        for peer in peers:
            pl.semaphore_signal(barrier, 1, device_id={axis: peer}, device_id_type=MESH)

    def share(axis, slot, peers, source_ref, landing_ref):
        for peer in peers:
            pltpu.make_async_remote_copy(
                src_ref=source_ref,
                dst_ref=landing_ref,
                send_sem=send_sem.at[slot],
                recv_sem=recv_sem.at[slot],
                device_id={axis: peer},
                device_id_type=MESH,
            ).start()

    def arrived(slot, landing, sem=None):
        sem = recv_sem if sem is None else sem
        pltpu.make_async_copy(landing, landing, sem.at[slot]).wait()

    def others(landing):
        return landing.at[pl.ds(0, landing.shape[0] - 1)]

    def rows(b):
        return pl.ds(b * Y_PITCH, LANES)

    def across(y):
        return pl.ds(y, blocks, stride=Y_PITCH)

    def level(z):
        return pl.ds(z, nx, stride=pitch)

    def plane_step(i):
        return pl.ds(i * pitch, nz)

    z_state = [jnp.ones((nx, LANES), jnp.float32)] * 4
    z_steps = []

    def z_invert(z):
        z_rate[z] = 1.0 / vertical[:, z]

    def z_sweep(z):
        phi, phi_step, psi, psi_step = z_state
        back = nz - 1 - z
        z_phi[z] = phi
        z_psi[back] = psi
        phi_flux, psi_flux = phi * z_rate[z], psi * z_rate[back]
        z_first[z] = phi_flux
        z_second[back] = psi_flux
        phi_step = phi_step + phi_flux
        psi_step = psi_step + psi_flux
        z_state[:] = [phi + phi_step, phi_step, psi + psi_step, psi_step]

    def z_solve(z_inv, read, write):
        def keep(z, value=None):
            if value is None:
                return x_part2[pl.ds(z * nx, nx)]
            x_part2[pl.ds(z * nx, nx)] = value

        return running(
            nz, lambda z: z_first[z], lambda z: z_second[z], read, lambda z: z_phi[z], lambda z: z_psi[z],
            z_inv, keep, write,
        )

    def z_first_solve():
        z_hold[...] = 1.0 / z_state[0]

        def to_plane(z, value):
            plane[level(z)] = value

        z_steps.extend(z_solve(z_hold[...], lambda z: source[:, z], to_plane))
        z_steps.extend(functools.partial(y_turn, b) for b in range(blocks))

    def y_turn(b):
        y_value[rows(b)] = jnp.concatenate(
            [plane[plane_step(b * wide + i)] for i in range(wide)], axis=0
        ).T

    for z in range(nz // 2):
        for at in (z, nz - 1 - z):
            z_steps.append(functools.partial(z_invert, at))
    z_steps.extend(functools.partial(z_sweep, z) for z in range(nz))
    z_steps.append(z_first_solve)

    for copy in loads[:3]:
        copy.wait()
    for b in range(blocks):
        y_rate[rows(b)] = (1.0 / north[b * LANES:(b + 1) * LANES]).T

    unit = jnp.ones((blocks, LANES), jnp.float32)
    phi, phi_step, psi, psi_step = unit, unit, unit, unit
    for i in range(LANES):
        back = LANES - 1 - i
        y_phi[across(i)] = phi
        y_psi[across(back)] = psi
        phi_flux, psi_flux = phi * y_rate[across(i)], psi * y_rate[across(back)]
        y_first[across(i)] = phi_flux
        y_second[across(back)] = psi_flux
        phi_step = phi_step + phi_flux
        psi_step = psi_step + psi_flux
        phi = phi + phi_step
        psi = psi + psi_step
        if z_steps and i % 16 < 10:
            z_steps.pop(0)()
    while z_steps:
        z_steps.pop(0)()
    y_inv = 1.0 / phi
    hold[pl.ds(2 * blocks, blocks)] = y_inv
    y_coef[pl_me, 0] = y_psi[across(0)] * y_inv
    y_coef[pl_me, 1] = y_phi[across(LANES - 1)] * y_inv
    y_coef[pl_me, 2] = y_inv

    low = lax.broadcasted_iota(jnp.int32, (LANES, LANES), 0)
    high = lax.broadcasted_iota(jnp.int32, (LANES, LANES), 1)
    upto = jnp.where(high <= low, 1.0, 0.0)
    beyond = jnp.where(high > low, 1.0, 0.0)

    def y_inv_row(b):
        return hold[2 * blocks + b:2 * blocks + b + 1]

    def y_ends_of(ends):
        for b in range(blocks):
            value = y_value[rows(b)]
            second = y_second[rows(b)] * value
            first = y_first[rows(b)] * value
            y_value[rows(b)] = first
            y_part[rows(b)] = second
            ends[pl_me, 0, b:b + 1] = jnp.sum(second, axis=0, keepdims=True) * y_inv_row(b)
            ends[pl_me, 1, b:b + 1] = jnp.sum(first, axis=0, keepdims=True) * y_inv_row(b)

    def y_local():
        for b in range(blocks):
            below = jnp.dot(upto, y_value[rows(b)], precision=HIGHEST, preferred_element_type=jnp.float32)
            above = jnp.dot(beyond, y_part[rows(b)], precision=HIGHEST, preferred_element_type=jnp.float32)
            y_part[rows(b)] = (y_psi[rows(b)] * below + y_phi[rows(b)] * above) * y_inv_row(b)

    def y_finish(slot, ends):
        arrived(slot, others(ends))
        a = c = jnp.zeros((blocks, LANES), jnp.float32)
        y_scan[0, 0] = a
        y_scan[1, n_pl] = c
        for j in range(n_pl):
            k = n_pl - 1 - j
            a = ends[j, 1] + y_fac[2, j] * ends[j, 0] + y_fac[1, j] * a
            c = ends[k, 0] + y_fac[4, k] * ends[k, 1] + y_fac[3, k] * c
            y_scan[0, j + 1] = a
            y_scan[1, k] = c
        a_here, a_next = y_scan[0, pl_me], y_scan[0, pl_me + 1]
        c_here, c_next = y_scan[1, pl_me], y_scan[1, pl_me + 1]
        outside_low = (a_here + y_fac[0, pl_me] * c_here) * y_fac[6, pl_me]
        outside_high = (c_next + y_fac[5, pl_me + 1] * a_next) * y_fac[6, pl_me + 1]
        inv = y_coef[pl_me, 2]
        hold[pl.ds(0, blocks)] = outside_low * inv
        hold[pl.ds(blocks, blocks)] = outside_high * inv
        for b in range(blocks):
            solved = (
                y_part[rows(b)]
                + y_psi[rows(b)] * hold[b:b + 1]
                + y_phi[rows(b)] * hold[blocks + b:blocks + b + 1]
            )
            solved = solved.T
            for i in range(wide):
                plane[plane_step(b * wide + i)] = solved[i * nz:(i + 1) * nz]

    y_ends_of(y_ends)

    def step(i):
        return pl.ds(i * nz, nz)

    loads[3].wait()
    phi = jnp.ones((nz, LANES), jnp.float32)
    phi_step = psi = psi_step = phi
    for i in range(nx // 2):
        for at in (i, nx - 1 - i):
            east[step(at)] = 1.0 / east[step(at)]
    for i in range(nx):
        back = nx - 1 - i
        x_phi[step(i)] = phi
        x_psi[step(back)] = psi
        phi_flux, psi_flux = phi * east[step(i)], psi * east[step(back)]
        x_first[step(i)] = phi_flux
        x_second[step(back)] = psi_flux
        phi_step = phi_step + phi_flux
        psi_step = psi_step + psi_flux
        phi = phi + phi_step
        psi = psi + psi_step
    x_inv = 1.0 / phi

    def x_solve(read, write, spare=None):
        spare = x_part2 if spare is None else spare

        def keep(i, value=None):
            if value is None:
                return spare[step(i)]
            spare[step(i)] = value

        return running(
            nx, lambda i: x_first[step(i)], lambda i: x_second[step(i)], read,
            lambda i: x_phi[step(i)], lambda i: x_psi[step(i)], x_inv, keep, write,
        )

    def into(ref):
        def write(i, value):
            ref[step(i)] = value

        return write

    for one, two in zip(
        x_solve(lambda i: x_phi[step(i)], into(x_phi2)),
        x_solve(lambda i: x_psi[step(i)], into(x_psi2), x_part),
    ):
        one()
        two()
    for i in range(nx):
        x_first2[step(i)] = x_phi2[step(i)] * east[step(i)]
        x_second2[step(i)] = x_psi2[step(i)] * east[step(i)]
    last = step(nx - 1)
    coefficients = (
        x_psi[step(0)] * x_inv, x_phi[last] * x_inv, x_inv,
        x_psi2[step(0)] * x_inv, x_phi2[last] * x_inv, x_phi2[step(0)] * x_inv,
    )
    for q, value in enumerate(coefficients):
        x_coef[0, q] = value[:half]
        x_coef[1, q] = value[half:]
    x_two_coef[core] = x_coef[core]
    pl.semaphore_wait(barrier, n_pl + chips - 1)
    share("xs", 2, mate, x_coef.at[other], x_two_coef.at[core])
    share("pl", 0, pl_peers, y_coef.at[pl_me], y_coef.at[pl_me])
    share("pl", 1, pl_peers, y_ends.at[pl_me], y_ends.at[pl_me])

    y_local()

    arrived(2, x_two_coef.at[0])
    left_a, right_a, shared_a, left2_a, right2_a, shared2_a = (x_two_coef[0, q] for q in range(6))
    left_b, right_b, shared_b, left2_b, right2_b, shared2_b = (x_two_coef[1, q] for q in range(6))
    meet = 1.0 / (1.0 - right_a * left_b)
    last_low, last_high = meet * shared_a, meet * right_a * shared_b
    first_low, first_high = meet * left_b * shared_a, meet * shared_b
    x_meet[0] = meet
    for q, value in enumerate((last_low, last_high, first_low, first_high)):
        x_meet[q + 1] = value

    def joined(p0a, pna, p0b, pnb):
        return (
            p0a + shared_a * (meet * (p0b + left_b * pna)),
            pnb + shared_b * (meet * (pna + right_a * p0b)),
        )

    first_from_low, _ = joined(
        left2_a + shared2_a * first_low, shared2_a + right2_a * first_low,
        left2_b * last_low, shared2_b * last_low,
    )
    first_from_high, last_from_high = joined(
        shared2_a * first_high, right2_a * first_high,
        left2_b * last_high + shared2_b, shared2_b * last_high + right2_b,
    )
    merged = (
        left_a + shared_a * first_low, right_b + shared_b * last_high, shared_a * first_high,
        first_from_low, last_from_high, first_from_high,
    )
    for q, value in enumerate(merged):
        x_chip_coef[chip, q] = value
    share("xs", 3, ring_peers, x_chip_coef.at[chip], x_chip_coef.at[chip])

    names = {"b": 0, "a1": 1, "a2": 2, "c1": 3, "c2": 4, "d": 5, "g": 6}
    arrived(0, others(y_coef))

    def y_store(name, j, value):
        y_fac[names[name], j] = value

    reduced_factors(n_pl, lambda j: (y_coef[j, 0], y_coef[j, 1], y_coef[j, 2]), y_store)
    y_finish(1, y_ends)

    p0 = pn = q0 = qn = jnp.zeros((nz, LANES), jnp.float32)
    for i in range(nx):
        value = plane[plane_step(i)]
        p0 = p0 + x_second[step(i)] * value
        pn = pn + x_first[step(i)] * value
        q0 = q0 + x_second2[step(i)] * value
        qn = qn + x_first2[step(i)] * value
    for q, value in enumerate((p0, pn, q0, qn)):
        x_ends[0, q] = value[:half] * x_inv[:half]
        x_ends[1, q] = value[half:] * x_inv[half:]
    share("xs", 4, mate, x_ends.at[other], x_two.at[core])
    x_two[core] = x_ends[core]

    for run in x_solve(lambda i: plane[plane_step(i)], into(x_part)):
        run()

    arrived(4, x_two.at[0])
    left_a, right_a, shared_a, left2_a, right2_a, shared2_a = (x_two_coef[0, q] for q in range(6))
    left_b, right_b, shared_b, left2_b, right2_b, shared2_b = (x_two_coef[1, q] for q in range(6))
    meet, last_low, last_high, first_low, first_high = (x_meet[q] for q in range(5))

    def border(p0b, pna):
        return meet * (pna + right_a * p0b), meet * (p0b + left_b * pna)

    def ends_again(last_a, first_b, low, high):
        p0a, pna = x_two[0, 2] + shared2_a * first_b, x_two[0, 3] + right2_a * first_b
        p0b, pnb = x_two[1, 2] + left2_b * last_a, x_two[1, 3] + shared2_b * last_a
        if low is not None:
            p0a, pna = p0a + left2_a * low, pna + shared2_a * low
            p0b, pnb = p0b + shared2_b * high, pnb + right2_b * high
        return p0a, pna, p0b, pnb

    last_a, first_b = border(x_two[1, 0], x_two[0, 1])
    x_chip[chip, 0] = x_two[0, 0] + shared_a * first_b
    x_chip[chip, 1] = x_two[1, 1] + shared_b * last_a
    p0a, pna, p0b, pnb = ends_again(last_a, first_b, None, None)
    last2, first2 = border(p0b, pna)
    x_chip[chip, 2] = p0a + shared_a * first2
    x_chip[chip, 3] = pnb + shared_b * last2
    share("xs", 5, ring_peers, x_chip.at[chip], x_chip.at[chip])

    arrived(3, others(x_chip_coef))

    def x_store(name, j, value):
        x_fac[names[name], j] = value

    reduced_factors(
        chips, lambda j: (x_chip_coef[j, 0], x_chip_coef[j, 1], x_chip_coef[j, 2]), x_store
    )
    for run in x_solve(lambda i: x_part[step(i)], into(x_part)):
        run()

    arrived(5, others(x_chip))

    def fac(name, j):
        return x_fac[names[name], j]

    def x_reduced(ends, only_here=False):
        a = c = jnp.zeros((half, LANES), jnp.float32)
        lefts, rights = [a], [c]
        for j in range(chips):
            k = chips - 1 - j
            a = ends[j][1] + fac("a2", j) * ends[j][0] + fac("a1", j) * a
            c = ends[k][0] + fac("c2", k) * ends[k][1] + fac("c1", k) * c
            lefts.append(a)
            rights.append(c)
        rights = rights[::-1]
        if only_here:
            for j in range(chips + 1):
                x_outside[j, 0] = lefts[j]
                x_outside[j, 1] = rights[j]
            here, after = chip, chip + 1
            return (
                (x_outside[here, 0] + x_fac[0, here] * x_outside[here, 1]) * x_fac[6, here],
                (x_outside[after, 1] + x_fac[5, after] * x_outside[after, 0]) * x_fac[6, after],
            )
        lows = [(lefts[j] + fac("b", j) * rights[j]) * fac("g", j) for j in range(chips)]
        highs = [
            (rights[j + 1] + fac("d", j + 1) * lefts[j + 1]) * fac("g", j + 1) for j in range(chips)
        ]
        return lows, highs

    lows, highs = x_reduced([(x_chip[j, 0], x_chip[j, 1]) for j in range(chips)])
    again = []
    for j in range(chips):
        left, right, shared = (x_chip_coef[j, q] for q in range(3, 6))
        again.append(
            (
                x_chip[j, 2] + left * lows[j] + shared * highs[j],
                x_chip[j, 3] + shared * lows[j] + right * highs[j],
            )
        )
    for j in range(chips):
        x_outside[j, 2] = lows[j]
        x_outside[j, 3] = highs[j]
    low2, high2 = x_reduced(again, only_here=True)
    low, high = x_outside[chip, 2], x_outside[chip, 3]
    last_a, first_b = border(x_two[1, 0], x_two[0, 1])
    last_a = last_a + last_low * low + last_high * high
    first_b = first_b + first_low * low + first_high * high
    p0a, pna, p0b, pnb = ends_again(last_a, first_b, low, high)
    last2, first2 = border(p0b, pna)
    last2 = last2 + last_low * low2 + last_high * high2
    first2 = first2 + first_low * low2 + first_high * high2
    for q, value in enumerate((low, first_b, low2, first2)):
        x_back[0, q] = value
    for q, value in enumerate((last_a, high, last2, high2)):
        x_back[1, q] = value
    share("xs", 6, mate, x_back.at[other], x_back_in.at[core])
    x_back_in[core] = x_back[core]

    arrived(6, x_back_in.at[0])
    low1, high1, low2, high2 = (
        jnp.concatenate([x_back_in[0, q], x_back_in[1, q]], axis=0) * x_inv for q in range(4)
    )
    for i in range(nx):
        plane[plane_step(i)] = (
            x_part[step(i)]
            + x_psi2[step(i)] * low1
            + x_phi2[step(i)] * high1
            + x_psi[step(i)] * low2
            + x_phi[step(i)] * high2
        )

    for b in range(blocks):
        y_turn(b)
    y_ends_of(y_ends2)
    share("pl", 7, pl_peers, y_ends2.at[pl_me], y_ends2.at[pl_me])
    y_local()
    y_finish(7, y_ends2)

    def to_out(z, value):
        out_ref[pl.ds(z, nx, stride=nz)] = value

    for run in z_solve(z_hold[...], lambda z: plane[level(z)], to_out):
        run()

    for slot, landing in enumerate(
        (
            others(y_coef), others(y_ends), x_two_coef.at[0], others(x_chip_coef),
            x_two.at[0], others(x_chip), x_back_in.at[0], others(y_ends2),
        )
    ):
        arrived(slot, landing, send_sem)


def shards(n_pl, n_xs, source, eastward_rate, northward_rate, vertical_rate, amplitude):
    nx, nz, ny = source.shape
    lines = nx * nz
    blocks = lines // LANES
    chips, half = n_xs // 2, nz // 2
    here = lambda array: pltpu.with_memory_space_constraint(array, pltpu.HBM)
    flat = lambda array: here(array.reshape(lines, ny))
    field = pltpu.VMEM((lines, LANES), jnp.float32)
    padded = pltpu.VMEM((nx, nz + Z_SPARE, LANES), jnp.float32)
    turned = pltpu.VMEM((blocks * Y_PITCH, LANES), jnp.float32)
    column = pltpu.VMEM((nz, nx, LANES), jnp.float32)
    vmem = lambda *shape: pltpu.VMEM(shape, jnp.float32)
    second = pl.pallas_call(
        functools.partial(kernel, nx, nz, n_pl, n_xs),
        out_shape=jax.ShapeDtypeStruct((lines, ny), jnp.float32),
        in_specs=[pl.BlockSpec(memory_space=pltpu.HBM)] * 4,
        out_specs=pl.BlockSpec(memory_space=pltpu.VMEM),
        scratch_shapes=[padded, padded, field, field]
        + [column] * 5
        + [vmem(nx, LANES)]
        + [turned] * 7
        + [field] * 8
        + [field] * 2
        + [vmem(nx * (nz + Z_SPARE), LANES)]
        + [vmem(3 * blocks, LANES)]
        + [
            vmem(n_pl, 3, blocks, LANES),
            vmem(n_pl, 2, blocks, LANES),
            vmem(n_pl, 2, blocks, LANES),
            vmem(2, 6, half, LANES),
            vmem(2, 6, half, LANES),
            vmem(chips, 6, half, LANES),
            vmem(2, 4, half, LANES),
            vmem(2, 4, half, LANES),
            vmem(chips, 4, half, LANES),
            vmem(chips + 1, 4, half, LANES),
            vmem(2, 4, half, LANES),
            vmem(2, 4, half, LANES),
            vmem(5, half, LANES),
            vmem(7, n_pl + 1, blocks, LANES),
            vmem(2, n_pl + 1, blocks, LANES),
            vmem(7, chips + 1, half, LANES),
            pltpu.SemaphoreType.DMA((4,)),
            pltpu.SemaphoreType.DMA((8,)),
            pltpu.SemaphoreType.DMA((8,)),
        ],
        compiler_params=pltpu.CompilerParams(
            collective_id=0, has_side_effects=True, vmem_limit_bytes=40 * 1024 * 1024
        ),
        name="adi",
    )(here(source), here(vertical_rate), flat(northward_rate), flat(eastward_rate))
    return amplitude * second.reshape(nx, nz, ny)


def solution(mesh):
    spec = P("xs", None, "pl")
    return jax.shard_map(
        functools.partial(shards, mesh.shape["pl"], mesh.shape["xs"]),
        mesh=mesh,
        in_specs=(spec,) * 5,
        out_specs=spec,
        check_vma=False,
    )
```

```python
import functools
import math

import jax
import jax.numpy as jnp
from jax import lax
from jax.experimental import pallas as pl
from jax.experimental.pallas import tpu as pltpu
from jax.sharding import PartitionSpec as P

MESH = pl.DeviceIdType.MESH
LANES = 128
Y_PITCH = LANES + 8
Z_SPARE = 8
HIGHEST = lax.Precision.HIGHEST


def reduced_factors(count, load, store):
    one = None
    b = None
    forward = []
    for j in range(count):
        left, right, shared = load(j)
        if b is None:
            b = jnp.zeros_like(left)
            one = jnp.ones_like(left)
        store("b", j, b)
        a1 = shared / (one - left * b)
        a2 = a1 * b
        store("a1", j, a1)
        store("a2", j, a2)
        b = right + a2 * shared
        forward.append(b)
    store("b", count, b)
    d = jnp.zeros_like(b)
    store("d", count, d)
    store("g", count, one)
    for j in reversed(range(count)):
        left, right, shared = load(j)
        c1 = shared / (one - right * d)
        c2 = c1 * d
        store("c1", j, c1)
        store("c2", j, c2)
        d = left + c2 * shared
        store("d", j, d)
        before = forward[j - 1] if j else jnp.zeros_like(d)
        store("g", j, one / (one - before * d))


def running(count, first, second, value, phi, psi, scale, keep, emit):
    total = [None]

    def down(i):
        if i == count - 1:
            total[0] = jnp.zeros_like(scale)
        keep(i, total[0])
        total[0] = total[0] + second(i) * value(i)

    def up(i):
        if i == 0:
            total[0] = jnp.zeros_like(scale)
        total[0] = total[0] + first(i) * value(i)
        emit(i, scale * (psi(i) * total[0] + phi(i) * keep(i)))

    downs = [functools.partial(down, i) for i in reversed(range(count))]
    return downs + [functools.partial(up, i) for i in range(count)]


def kernel(
    nx, nz, n_pl, n_xs,
    source_hbm, vertical_hbm, north_hbm, east_hbm, out_ref,
    source, vertical, north, east,
    z_phi, z_psi, z_first, z_second, z_rate, z_hold,
    y_rate, y_phi, y_psi, y_first, y_second, y_value, y_part,
    x_phi, x_psi, x_phi2, x_psi2, x_first, x_second, x_first2, x_second2,
    x_part, x_part2, plane, hold,
    y_coef, y_ends, y_ends2, x_coef, x_two_coef, x_chip_coef, x_ends, x_two, x_chip,
    x_outside, x_back, x_back_in, x_meet, y_fac, y_scan, x_fac,
    load_sem, send_sem, recv_sem,
):
    lines = nx * nz
    blocks = lines // LANES
    pitch, wide = nz + Z_SPARE, LANES // nz
    pl_me, xs_me = lax.axis_index("pl"), lax.axis_index("xs")

    loads = []
    for slot, (hbm, vmem) in enumerate(
        ((north_hbm, north), (vertical_hbm, vertical), (source_hbm, source), (east_hbm, east))
    ):
        vmem = vmem.at[:, pl.ds(0, nz)] if len(vmem.shape) == 3 else vmem
        copy = pltpu.make_async_copy(hbm, vmem, load_sem.at[slot])
        copy.start()
        loads.append(copy)

    side, chips, half = math.isqrt(n_pl), n_xs // 2, nz // 2
    pl_row, pl_col = pl_me // side, lax.rem(pl_me, side)
    chip, core = xs_me // 2, lax.rem(xs_me, 2)
    other = 1 - core

    def ring(offset, count):
        return min(offset, count - offset)

    steps = [(r, c) for r in range(side) for c in range(side) if r or c]
    steps.sort(key=lambda step: -ring(step[0], side) - ring(step[1], side))
    pl_peers = [lax.rem(pl_row + r, side) * side + lax.rem(pl_col + c, side) for r, c in steps]
    ring_offsets = sorted(range(1, chips), key=lambda offset: -ring(offset, chips))
    ring_peers = [lax.rem(chip + offset, chips) * 2 + core for offset in ring_offsets]
    mate = [chip * 2 + other]

    barrier = pltpu.get_barrier_semaphore()
    for axis, peers in (
        ("pl", pl_peers[:5]), ("xs", ring_peers[:3]), ("pl", pl_peers[5:]), ("xs", ring_peers[3:] + mate),
    ):
        for peer in peers:
            pl.semaphore_signal(barrier, 1, device_id={axis: peer}, device_id_type=MESH)

    def share(axis, slot, peers, source_ref, landing_ref):
        for peer in peers:
            pltpu.make_async_remote_copy(
                src_ref=source_ref,
                dst_ref=landing_ref,
                send_sem=send_sem.at[slot],
                recv_sem=recv_sem.at[slot],
                device_id={axis: peer},
                device_id_type=MESH,
            ).start()

    def arrived(slot, landing, sem=None):
        sem = recv_sem if sem is None else sem
        pltpu.make_async_copy(landing, landing, sem.at[slot]).wait()

    def others(landing):
        return landing.at[pl.ds(0, landing.shape[0] - 1)]

    def rows(b):
        return pl.ds(b * Y_PITCH, LANES)

    def across(y):
        return pl.ds(y, blocks, stride=Y_PITCH)

    def level(z):
        return pl.ds(z, nx, stride=pitch)

    def plane_step(i):
        return pl.ds(i * pitch, nz)

    z_state = [jnp.ones((nx, LANES), jnp.float32)] * 4
    z_steps = []

    def z_invert(z):
        z_rate[z] = 1.0 / vertical[:, z]

    def z_sweep(z):
        phi, phi_step, psi, psi_step = z_state
        back = nz - 1 - z
        z_phi[z] = phi
        z_psi[back] = psi
        phi_flux, psi_flux = phi * z_rate[z], psi * z_rate[back]
        z_first[z] = phi_flux
        z_second[back] = psi_flux
        phi_step = phi_step + phi_flux
        psi_step = psi_step + psi_flux
        z_state[:] = [phi + phi_step, phi_step, psi + psi_step, psi_step]

    def z_solve(z_inv, read, write):
        def keep(z, value=None):
            if value is None:
                return x_part2[pl.ds(z * nx, nx)]
            x_part2[pl.ds(z * nx, nx)] = value

        return running(
            nz, lambda z: z_first[z], lambda z: z_second[z], read, lambda z: z_phi[z], lambda z: z_psi[z],
            z_inv, keep, write,
        )

    def z_first_solve():
        z_hold[...] = 1.0 / z_state[0]

        def to_plane(z, value):
            plane[level(z)] = value

        z_steps.extend(z_solve(z_hold[...], lambda z: source[:, z], to_plane))
        z_steps.extend(functools.partial(y_turn, b) for b in range(blocks))

    def y_turn(b):
        y_value[rows(b)] = jnp.concatenate(
            [plane[plane_step(b * wide + i)] for i in range(wide)], axis=0
        ).T

    for z in range(nz // 2):
        for at in (z, nz - 1 - z):
            z_steps.append(functools.partial(z_invert, at))
    z_steps.extend(functools.partial(z_sweep, z) for z in range(nz))
    z_steps.append(z_first_solve)

    for copy in loads[:3]:
        copy.wait()
    for b in range(blocks):
        y_rate[rows(b)] = (1.0 / north[b * LANES:(b + 1) * LANES]).T

    unit = jnp.ones((blocks, LANES), jnp.float32)
    phi, phi_step, psi, psi_step = unit, unit, unit, unit
    for i in range(LANES):
        back = LANES - 1 - i
        y_phi[across(i)] = phi
        y_psi[across(back)] = psi
        phi_flux, psi_flux = phi * y_rate[across(i)], psi * y_rate[across(back)]
        y_first[across(i)] = phi_flux
        y_second[across(back)] = psi_flux
        phi_step = phi_step + phi_flux
        psi_step = psi_step + psi_flux
        phi = phi + phi_step
        psi = psi + psi_step
        if z_steps and i % 16 < 10:
            z_steps.pop(0)()
    while z_steps:
        z_steps.pop(0)()
    y_inv = 1.0 / phi
    hold[pl.ds(2 * blocks, blocks)] = y_inv
    y_coef[pl_me, 0] = y_psi[across(0)] * y_inv
    y_coef[pl_me, 1] = y_phi[across(LANES - 1)] * y_inv
    y_coef[pl_me, 2] = y_inv

    low = lax.broadcasted_iota(jnp.int32, (LANES, LANES), 0)
    high = lax.broadcasted_iota(jnp.int32, (LANES, LANES), 1)
    upto = jnp.where(high <= low, 1.0, 0.0)
    beyond = jnp.where(high > low, 1.0, 0.0)

    def y_inv_row(b):
        return hold[2 * blocks + b:2 * blocks + b + 1]

    def y_ends_of(ends):
        for b in range(blocks):
            value = y_value[rows(b)]
            second = y_second[rows(b)] * value
            first = y_first[rows(b)] * value
            y_value[rows(b)] = first
            y_part[rows(b)] = second
            ends[pl_me, 0, b:b + 1] = jnp.sum(second, axis=0, keepdims=True) * y_inv_row(b)
            ends[pl_me, 1, b:b + 1] = jnp.sum(first, axis=0, keepdims=True) * y_inv_row(b)

    def y_local():
        for b in range(blocks):
            below = jnp.dot(upto, y_value[rows(b)], precision=HIGHEST, preferred_element_type=jnp.float32)
            above = jnp.dot(beyond, y_part[rows(b)], precision=HIGHEST, preferred_element_type=jnp.float32)
            y_part[rows(b)] = (y_psi[rows(b)] * below + y_phi[rows(b)] * above) * y_inv_row(b)

    def y_finish(slot, ends):
        arrived(slot, others(ends))
        a = c = jnp.zeros((blocks, LANES), jnp.float32)
        y_scan[0, 0] = a
        y_scan[1, n_pl] = c
        for j in range(n_pl):
            k = n_pl - 1 - j
            a = ends[j, 1] + y_fac[2, j] * ends[j, 0] + y_fac[1, j] * a
            c = ends[k, 0] + y_fac[4, k] * ends[k, 1] + y_fac[3, k] * c
            y_scan[0, j + 1] = a
            y_scan[1, k] = c
        a_here, a_next = y_scan[0, pl_me], y_scan[0, pl_me + 1]
        c_here, c_next = y_scan[1, pl_me], y_scan[1, pl_me + 1]
        outside_low = (a_here + y_fac[0, pl_me] * c_here) * y_fac[6, pl_me]
        outside_high = (c_next + y_fac[5, pl_me + 1] * a_next) * y_fac[6, pl_me + 1]
        inv = y_coef[pl_me, 2]
        hold[pl.ds(0, blocks)] = outside_low * inv
        hold[pl.ds(blocks, blocks)] = outside_high * inv
        for b in range(blocks):
            solved = (
                y_part[rows(b)]
                + y_psi[rows(b)] * hold[b:b + 1]
                + y_phi[rows(b)] * hold[blocks + b:blocks + b + 1]
            )
            solved = solved.T
            for i in range(wide):
                plane[plane_step(b * wide + i)] = solved[i * nz:(i + 1) * nz]

    y_ends_of(y_ends)

    def step(i):
        return pl.ds(i * nz, nz)

    loads[3].wait()
    phi = jnp.ones((nz, LANES), jnp.float32)
    phi_step = psi = psi_step = phi
    for i in range(nx // 2):
        for at in (i, nx - 1 - i):
            east[step(at)] = 1.0 / east[step(at)]
    for i in range(nx):
        back = nx - 1 - i
        x_phi[step(i)] = phi
        x_psi[step(back)] = psi
        phi_flux, psi_flux = phi * east[step(i)], psi * east[step(back)]
        x_first[step(i)] = phi_flux
        x_second[step(back)] = psi_flux
        phi_step = phi_step + phi_flux
        psi_step = psi_step + psi_flux
        phi = phi + phi_step
        psi = psi + psi_step
    x_inv = 1.0 / phi

    def x_solve(read, write, spare=None):
        spare = x_part2 if spare is None else spare

        def keep(i, value=None):
            if value is None:
                return spare[step(i)]
            spare[step(i)] = value

        return running(
            nx, lambda i: x_first[step(i)], lambda i: x_second[step(i)], read,
            lambda i: x_phi[step(i)], lambda i: x_psi[step(i)], x_inv, keep, write,
        )

    def into(ref):
        def write(i, value):
            ref[step(i)] = value

        return write

    for one, two in zip(
        x_solve(lambda i: x_phi[step(i)], into(x_phi2)),
        x_solve(lambda i: x_psi[step(i)], into(x_psi2), x_part),
    ):
        one()
        two()
    for i in range(nx):
        x_first2[step(i)] = x_phi2[step(i)] * east[step(i)]
        x_second2[step(i)] = x_psi2[step(i)] * east[step(i)]
    last = step(nx - 1)
    coefficients = (
        x_psi[step(0)] * x_inv, x_phi[last] * x_inv, x_inv,
        x_psi2[step(0)] * x_inv, x_phi2[last] * x_inv, x_phi2[step(0)] * x_inv,
    )
    for q, value in enumerate(coefficients):
        x_coef[0, q] = value[:half]
        x_coef[1, q] = value[half:]
    x_two_coef[core] = x_coef[core]
    pl.semaphore_wait(barrier, n_pl + chips - 1)
    share("xs", 2, mate, x_coef.at[other], x_two_coef.at[core])
    share("pl", 0, pl_peers, y_coef.at[pl_me], y_coef.at[pl_me])
    share("pl", 1, pl_peers, y_ends.at[pl_me], y_ends.at[pl_me])

    y_local()

    arrived(2, x_two_coef.at[0])
    left_a, right_a, shared_a, left2_a, right2_a, shared2_a = (x_two_coef[0, q] for q in range(6))
    left_b, right_b, shared_b, left2_b, right2_b, shared2_b = (x_two_coef[1, q] for q in range(6))
    meet = 1.0 / (1.0 - right_a * left_b)
    last_low, last_high = meet * shared_a, meet * right_a * shared_b
    first_low, first_high = meet * left_b * shared_a, meet * shared_b
    x_meet[0] = meet
    for q, value in enumerate((last_low, last_high, first_low, first_high)):
        x_meet[q + 1] = value

    def joined(p0a, pna, p0b, pnb):
        return (
            p0a + shared_a * (meet * (p0b + left_b * pna)),
            pnb + shared_b * (meet * (pna + right_a * p0b)),
        )

    first_from_low, _ = joined(
        left2_a + shared2_a * first_low, shared2_a + right2_a * first_low,
        left2_b * last_low, shared2_b * last_low,
    )
    first_from_high, last_from_high = joined(
        shared2_a * first_high, right2_a * first_high,
        left2_b * last_high + shared2_b, shared2_b * last_high + right2_b,
    )
    merged = (
        left_a + shared_a * first_low, right_b + shared_b * last_high, shared_a * first_high,
        first_from_low, last_from_high, first_from_high,
    )
    for q, value in enumerate(merged):
        x_chip_coef[chip, q] = value
    share("xs", 3, ring_peers, x_chip_coef.at[chip], x_chip_coef.at[chip])

    names = {"b": 0, "a1": 1, "a2": 2, "c1": 3, "c2": 4, "d": 5, "g": 6}
    arrived(0, others(y_coef))

    def y_store(name, j, value):
        y_fac[names[name], j] = value

    reduced_factors(n_pl, lambda j: (y_coef[j, 0], y_coef[j, 1], y_coef[j, 2]), y_store)
    y_finish(1, y_ends)

    p0 = pn = q0 = qn = jnp.zeros((nz, LANES), jnp.float32)
    for i in range(nx):
        value = plane[plane_step(i)]
        p0 = p0 + x_second[step(i)] * value
        pn = pn + x_first[step(i)] * value
        q0 = q0 + x_second2[step(i)] * value
        qn = qn + x_first2[step(i)] * value
    for q, value in enumerate((p0, pn, q0, qn)):
        x_ends[0, q] = value[:half] * x_inv[:half]
        x_ends[1, q] = value[half:] * x_inv[half:]
    share("xs", 4, mate, x_ends.at[other], x_two.at[core])
    x_two[core] = x_ends[core]

    for run in x_solve(lambda i: plane[plane_step(i)], into(x_part)):
        run()

    arrived(4, x_two.at[0])
    left_a, right_a, shared_a, left2_a, right2_a, shared2_a = (x_two_coef[0, q] for q in range(6))
    left_b, right_b, shared_b, left2_b, right2_b, shared2_b = (x_two_coef[1, q] for q in range(6))
    meet, last_low, last_high, first_low, first_high = (x_meet[q] for q in range(5))

    def border(p0b, pna):
        return meet * (pna + right_a * p0b), meet * (p0b + left_b * pna)

    def ends_again(last_a, first_b, low, high):
        p0a, pna = x_two[0, 2] + shared2_a * first_b, x_two[0, 3] + right2_a * first_b
        p0b, pnb = x_two[1, 2] + left2_b * last_a, x_two[1, 3] + shared2_b * last_a
        if low is not None:
            p0a, pna = p0a + left2_a * low, pna + shared2_a * low
            p0b, pnb = p0b + shared2_b * high, pnb + right2_b * high
        return p0a, pna, p0b, pnb

    last_a, first_b = border(x_two[1, 0], x_two[0, 1])
    x_chip[chip, 0] = x_two[0, 0] + shared_a * first_b
    x_chip[chip, 1] = x_two[1, 1] + shared_b * last_a
    p0a, pna, p0b, pnb = ends_again(last_a, first_b, None, None)
    last2, first2 = border(p0b, pna)
    x_chip[chip, 2] = p0a + shared_a * first2
    x_chip[chip, 3] = pnb + shared_b * last2
    share("xs", 5, ring_peers, x_chip.at[chip], x_chip.at[chip])

    arrived(3, others(x_chip_coef))

    def x_store(name, j, value):
        x_fac[names[name], j] = value

    reduced_factors(
        chips, lambda j: (x_chip_coef[j, 0], x_chip_coef[j, 1], x_chip_coef[j, 2]), x_store
    )
    for run in x_solve(lambda i: x_part[step(i)], into(x_part)):
        run()

    arrived(5, others(x_chip))

    def fac(name, j):
        return x_fac[names[name], j]

    def x_reduced(ends):
        a = c = jnp.zeros((half, LANES), jnp.float32)
        lefts, rights = [a], [c]
        for j in range(chips):
            k = chips - 1 - j
            a = ends[j][1] + fac("a2", j) * ends[j][0] + fac("a1", j) * a
            c = ends[k][0] + fac("c2", k) * ends[k][1] + fac("c1", k) * c
            lefts.append(a)
            rights.append(c)
        rights = rights[::-1]
        lows = [(lefts[j] + fac("b", j) * rights[j]) * fac("g", j) for j in range(chips)]
        highs = [
            (rights[j + 1] + fac("d", j + 1) * lefts[j + 1]) * fac("g", j + 1) for j in range(chips)
        ]
        return lows, highs

    lows, highs = x_reduced([(x_chip[j, 0], x_chip[j, 1]) for j in range(chips)])
    again = []
    for j in range(chips):
        left, right, shared = (x_chip_coef[j, q] for q in range(3, 6))
        again.append(
            (
                x_chip[j, 2] + left * lows[j] + shared * highs[j],
                x_chip[j, 3] + shared * lows[j] + right * highs[j],
            )
        )
    lows2, highs2 = x_reduced(again)
    for j in range(chips):
        for q, value in enumerate((lows[j], highs[j], lows2[j], highs2[j])):
            x_outside[j, q] = value
    low, high, low2, high2 = (x_outside[chip, q] for q in range(4))
    last_a, first_b = border(x_two[1, 0], x_two[0, 1])
    last_a = last_a + last_low * low + last_high * high
    first_b = first_b + first_low * low + first_high * high
    p0a, pna, p0b, pnb = ends_again(last_a, first_b, low, high)
    last2, first2 = border(p0b, pna)
    last2 = last2 + last_low * low2 + last_high * high2
    first2 = first2 + first_low * low2 + first_high * high2
    for q, value in enumerate((low, first_b, low2, first2)):
        x_back[0, q] = value
    for q, value in enumerate((last_a, high, last2, high2)):
        x_back[1, q] = value
    share("xs", 6, mate, x_back.at[other], x_back_in.at[core])
    x_back_in[core] = x_back[core]

    arrived(6, x_back_in.at[0])
    low1, high1, low2, high2 = (
        jnp.concatenate([x_back_in[0, q], x_back_in[1, q]], axis=0) * x_inv for q in range(4)
    )
    for i in range(nx):
        plane[plane_step(i)] = (
            x_part[step(i)]
            + x_psi2[step(i)] * low1
            + x_phi2[step(i)] * high1
            + x_psi[step(i)] * low2
            + x_phi[step(i)] * high2
        )

    for b in range(blocks):
        y_turn(b)
    y_ends_of(y_ends2)
    share("pl", 7, pl_peers, y_ends2.at[pl_me], y_ends2.at[pl_me])
    y_local()
    y_finish(7, y_ends2)

    def to_out(z, value):
        out_ref[pl.ds(z, nx, stride=nz)] = value

    for run in z_solve(z_hold[...], lambda z: plane[level(z)], to_out):
        run()

    for slot, landing in enumerate(
        (
            others(y_coef), others(y_ends), x_two_coef.at[0], others(x_chip_coef),
            x_two.at[0], others(x_chip), x_back_in.at[0], others(y_ends2),
        )
    ):
        arrived(slot, landing, send_sem)


def shards(n_pl, n_xs, source, eastward_rate, northward_rate, vertical_rate, amplitude):
    nx, nz, ny = source.shape
    lines = nx * nz
    blocks = lines // LANES
    chips, half = n_xs // 2, nz // 2
    here = lambda array: pltpu.with_memory_space_constraint(array, pltpu.HBM)
    flat = lambda array: here(array.reshape(lines, ny))
    field = pltpu.VMEM((lines, LANES), jnp.float32)
    padded = pltpu.VMEM((nx, nz + Z_SPARE, LANES), jnp.float32)
    turned = pltpu.VMEM((blocks * Y_PITCH, LANES), jnp.float32)
    column = pltpu.VMEM((nz, nx, LANES), jnp.float32)
    vmem = lambda *shape: pltpu.VMEM(shape, jnp.float32)
    second = pl.pallas_call(
        functools.partial(kernel, nx, nz, n_pl, n_xs),
        out_shape=jax.ShapeDtypeStruct((lines, ny), jnp.float32),
        in_specs=[pl.BlockSpec(memory_space=pltpu.HBM)] * 4,
        out_specs=pl.BlockSpec(memory_space=pltpu.VMEM),
        scratch_shapes=[padded, padded, field, field]
        + [column] * 5
        + [vmem(nx, LANES)]
        + [turned] * 7
        + [field] * 8
        + [field] * 2
        + [vmem(nx * (nz + Z_SPARE), LANES)]
        + [vmem(3 * blocks, LANES)]
        + [
            vmem(n_pl, 3, blocks, LANES),
            vmem(n_pl, 2, blocks, LANES),
            vmem(n_pl, 2, blocks, LANES),
            vmem(2, 6, half, LANES),
            vmem(2, 6, half, LANES),
            vmem(chips, 6, half, LANES),
            vmem(2, 4, half, LANES),
            vmem(2, 4, half, LANES),
            vmem(chips, 4, half, LANES),
            vmem(chips, 4, half, LANES),
            vmem(2, 4, half, LANES),
            vmem(2, 4, half, LANES),
            vmem(5, half, LANES),
            vmem(7, n_pl + 1, blocks, LANES),
            vmem(2, n_pl + 1, blocks, LANES),
            vmem(7, chips + 1, half, LANES),
            pltpu.SemaphoreType.DMA((4,)),
            pltpu.SemaphoreType.DMA((8,)),
            pltpu.SemaphoreType.DMA((8,)),
        ],
        compiler_params=pltpu.CompilerParams(
            collective_id=0, has_side_effects=True, vmem_limit_bytes=40 * 1024 * 1024
        ),
        name="adi",
    )(here(source), here(vertical_rate), flat(northward_rate), flat(eastward_rate))
    return amplitude * second.reshape(nx, nz, ny)


def solution(mesh):
    spec = P("xs", None, "pl")
    return jax.shard_map(
        functools.partial(shards, mesh.shape["pl"], mesh.shape["xs"]),
        mesh=mesh,
        in_specs=(spec,) * 5,
        out_specs=spec,
        check_vma=False,
    )
```
